32 devices in a mesh: seq: 16 (over z, y, core), head: 2 (over x).
Axes of the slice: x: 2, y: 2, z: 4, core: 2. Of those that a mesh axis runs over, the one named last changes fastest.
Arguments:
- queries: bfloat16 [2048, 3072], P('seq', 'head')
- block_keys: bfloat16 [2048, 3072], P('seq', 'head')
- block_values: bfloat16 [2048, 3072], P('seq', 'head'), may hold values from -6 to 6
- cache_keys: bfloat16 [256, 3072], P('seq', 'head'), may hold values from -6 to 6
- cache_values: bfloat16 [256, 3072], P('seq', 'head'), may hold values from -6 to 6
- cache_lengths: int32 [16], P('seq'), may hold values from 1 to 16
- out_weight: bfloat16 [3072, 5120], P('head'), may hold values from -0.15625 to 0.15625
Outputs:
- projected: bfloat16 [2048, 5120], P('seq', 'head')
The draws below stay inside these ranges and needn't reach their ends.
All inputs are finite; a program needn't handle non-finite values.
Results may differ from the reference program's by a relative error of at most 0.014.
Values may be sent and summed in bfloat16 or wider, within the bound.
No kernel may reach another device: no remote copies, remote signals or barrier semaphores. Data moves between devices by JAX's collectives and lax.ppermute only.
A program may use at most 128 MiB of HBM per device.

```python
import math
import jax
import jax.numpy as jnp
from jax import lax

HEADS = 24
DH = 128
D = 5120
KV_DEV = 16
BLOCK = 2048
CACHE = 256


def joint_query_keys(key):
    first_key, second_key = jax.random.split(jax.random.fold_in(key, 11))
    queries = jnp.clip(2.5 * jax.random.normal(first_key, (BLOCK, HEADS * DH), jnp.float32), -15.0, 15.0)
    keys_drawn = jnp.clip(jax.random.normal(second_key, (BLOCK, HEADS * DH), jnp.float32), -6.0, 6.0)
    return (queries, keys_drawn)


def draw_queries(key, part):
    return joint_query_keys(key)[0].astype(jnp.bfloat16)


def draw_block_keys(key, part):
    return joint_query_keys(key)[1].astype(jnp.bfloat16)


def draw_cache_lengths(key, part):
    first_key, second_key = jax.random.split(jax.random.fold_in(key, 23))
    shards = CACHE // KV_DEV
    drawn = jax.random.randint(first_key, (shards,), 1, KV_DEV + 1, dtype=jnp.int32)
    chosen = jax.random.randint(second_key, (), 0, shards, dtype=jnp.int32)
    return jnp.where(jnp.arange(shards, dtype=jnp.int32) == chosen, KV_DEV, drawn).astype(jnp.int32)


def spiked(values, stream_key, source, target, parts, factor):
    def block_of(dim):
        return (jnp.arange(values.shape[dim]) // (values.shape[dim] // parts)).reshape((-1,) + (1,) * (values.ndim - 1 - dim))

    near = jax.random.permutation(stream_key, parts)[block_of(target)]
    far = (block_of(target) + parts // 2) % parts
    return jnp.where((block_of(source) == near) | (block_of(source) == far), factor * values, values)


def steps_of(stream_key, shape, cuts, smallest, high):
    factor_of, own = 1.0, jax.random.fold_in(stream_key, 6)
    for dim, blocks in cuts:
        steps = jnp.exp(jax.random.uniform(jax.random.fold_in(own, dim), (blocks,), jnp.float32, smallest / len(cuts), high / len(cuts)))
        factor_of = factor_of * jnp.repeat(steps, shape[dim] // blocks).reshape([-1 if axis == dim else 1 for axis in range(len(shape))])
    return factor_of


def gaussian(key, shape, spread, bound, cuts=(), kind=jnp.bfloat16):
    values = spread * jax.random.normal(key, shape, jnp.float32)
    if cuts:
        values = values * steps_of(key, shape, cuts, -0.22, 0.18)
    return jnp.clip(values, -bound, bound).astype(kind)


def noise_with(own_key, shape, spread, reach, cuts, heavy, held_as=jnp.bfloat16):
    entries = spread * jax.random.normal(own_key, shape, jnp.float32)
    if cuts:
        entries = entries * steps_of(own_key, shape, cuts, -0.22, 0.18)
    return jnp.clip(spiked(entries, jax.random.fold_in(own_key, 3), *heavy), -reach, reach).astype(held_as)


def setup_inputs(seed: int = 0) -> dict:
    streams_of = jax.random.split(jax.random.key(seed), 8)
    return {
        "queries": draw_queries(jax.random.fold_in(streams_of[7], 71), 0),
        "block_keys": draw_block_keys(jax.random.fold_in(streams_of[7], 71), 0),
        "block_values": gaussian(streams_of[2], (BLOCK, HEADS * DH), 1.0, 6.0, ((0, 16), (1, 2))),
        "cache_keys": gaussian(streams_of[3], (CACHE, HEADS * DH), 1.0, 6.0, ((0, 16), (1, 2))),
        "cache_values": gaussian(streams_of[4], (CACHE, HEADS * DH), 1.0, 6.0, ((0, 16), (1, 2))),
        "cache_lengths": draw_cache_lengths(jax.random.fold_in(streams_of[7], 71), 0),
        "out_weight": noise_with(streams_of[6], (HEADS * DH, D), (HEADS * DH) ** -0.5, 0.15625, ((0, 2),), (0, 1, 2, 2.0)),
    }


NEG_BIG = -1e+30

def attend_head(query_head, key_head, value_head, usable):
    scores = jnp.dot(query_head, key_head.T, preferred_element_type=jnp.float32) * (1.0 / math.sqrt(DH))
    scores = jnp.where(usable[None, :], scores, NEG_BIG)
    maxima = lax.optimization_barrier(jnp.max(scores, axis=1, keepdims=True))
    weights = jnp.exp(scores - maxima)
    totals = lax.optimization_barrier(jnp.sum(weights, axis=1, keepdims=True))
    mixed = jnp.dot(weights.astype(jnp.bfloat16), value_head, preferred_element_type=jnp.float32)
    return (mixed / totals).astype(jnp.bfloat16)

def reference(queries, block_keys, block_values, cache_keys, cache_values, cache_lengths, out_weight):
    key_rows = jnp.concatenate([block_keys, cache_keys], axis=0)
    value_rows = jnp.concatenate([block_values, cache_values], axis=0)
    slot_index = jnp.arange(CACHE, dtype=jnp.int32) % KV_DEV
    slot_limit = jnp.repeat(cache_lengths.astype(jnp.int32), KV_DEV, total_repeat_length=CACHE)
    usable = jnp.concatenate([jnp.ones((BLOCK,), jnp.bool_), slot_index < slot_limit])
    query_heads = queries.reshape(BLOCK, HEADS, DH).transpose(1, 0, 2)
    key_heads = key_rows.reshape(BLOCK + CACHE, HEADS, DH).transpose(1, 0, 2)
    value_heads = value_rows.reshape(BLOCK + CACHE, HEADS, DH).transpose(1, 0, 2)
    mixed = lax.map(lambda triple: attend_head(triple[0], triple[1], triple[2], usable), (query_heads, key_heads, value_heads))
    attended = mixed.transpose(1, 0, 2).reshape(BLOCK, HEADS * DH)
    return jnp.dot(attended, out_weight, preferred_element_type=jnp.float32).astype(jnp.bfloat16)
```

```python
import functools
import math

import jax
import jax.numpy as jnp
from jax import lax
from jax.experimental import pallas as pl
from jax.experimental.pallas import tpu as pltpu
from jax.sharding import PartitionSpec as P

DH = 128
NEG_BIG = -1e30
CORES = 2
GROUPS = 4


def fold_keys(running, query_heads, key_rows, value_rows, usable):
    maxima, totals, accumulated = running
    heads_here = query_heads.shape[1]
    head_width = query_heads.shape[2]
    key_heads = key_rows.reshape(key_rows.shape[0], heads_here, head_width)
    value_heads = value_rows.reshape(value_rows.shape[0], heads_here, head_width)
    scores = jnp.einsum(
        "qhd,khd->hqk", query_heads, key_heads, preferred_element_type=jnp.float32
    ) * (1.0 / math.sqrt(head_width))
    if usable is not None:
        scores = jnp.where(usable[None, None, :], scores, NEG_BIG)
    newest = jnp.maximum(maxima, jnp.max(scores, axis=2))
    carried = jnp.exp(maxima - newest)
    weights = jnp.exp(scores - newest[:, :, None])
    totals = totals * carried + jnp.sum(weights, axis=2)
    mixed = jnp.einsum(
        "hqk,khd->hqd",
        weights.astype(jnp.bfloat16),
        value_heads,
        preferred_element_type=jnp.float32,
    )
    accumulated = accumulated * carried[:, :, None] + mixed
    return (newest, totals, accumulated)


def cache_usable(lengths_piece, slots, row_count):
    slot_index = jnp.arange(row_count, dtype=jnp.int32) % slots
    slot_limit = jnp.repeat(lengths_piece.astype(jnp.int32), slots, total_repeat_length=row_count)
    return slot_index < slot_limit


def gathered_plan(
    queries, block_keys, block_values, cache_keys, cache_values, cache_lengths, out_weight
):
    tokens_here = queries.shape[0]
    heads_here = queries.shape[1] // DH
    query_heads = queries.reshape(tokens_here, heads_here, DH)
    slots = cache_keys.shape[0]
    running = (
        jnp.full((heads_here, tokens_here), NEG_BIG, jnp.float32),
        jnp.zeros((heads_here, tokens_here), jnp.float32),
        jnp.zeros((heads_here, tokens_here, DH), jnp.float32),
    )
    gather = functools.partial(lax.all_gather, axis_name="seq", axis=0, tiled=True)
    running = fold_keys(running, query_heads, gather(block_keys), gather(block_values), None)
    cached = gather(cache_keys)
    usable = cache_usable(gather(cache_lengths), slots, cached.shape[0])
    running = fold_keys(running, query_heads, cached, gather(cache_values), usable)
    _, totals, accumulated = running
    attended = (
        (accumulated / totals[:, :, None])
        .transpose(1, 0, 2)
        .reshape(tokens_here, heads_here * DH)
        .astype(jnp.bfloat16)
    )
    partial_terms = jnp.dot(attended, out_weight, preferred_element_type=jnp.float32)
    return lax.psum_scatter(
        partial_terms.astype(jnp.bfloat16), "head", scatter_dimension=1, tiled=True
    )


def run_copies(copies, sems):
    started = [
        pltpu.make_async_copy(src, dst, sems.at[i]) for i, (src, dst) in enumerate(copies)
    ]
    for copy in started:
        copy.start()
    for copy in started:
        copy.wait()


def pack_kernel(seq, width, tokens, slots, len_ref, q, k, v, ck, cv, *refs):
    outs, (mask, sems) = refs[: 2 * GROUPS], refs[2 * GROUPS :]
    me = lax.div(lax.axis_index("seq"), seq // GROUPS)
    lane = lax.broadcasted_iota(jnp.int32, (16, width), 1)
    mask[...] = jnp.where(lax.rem(lane, slots) < len_ref[0], 1.0, 0.0).astype(jnp.bfloat16)
    copies = []
    for step in range(GROUPS):
        group = lax.bitwise_xor(me, step)
        cols = pl.ds(pl.multiple_of(group * width, width), width)
        kv, qo = outs[2 * step], outs[2 * step + 1]
        row = 0
        for src in (k, v, ck, cv):
            rows = src.shape[0]
            copies.append((src.at[:, cols], kv.at[pl.ds(row, rows), :]))
            row += rows
        copies.append((mask, kv.at[pl.ds(row, 16), :]))
        copies.append((q.at[:, cols], qo))
    run_copies(copies, sems)


def pack(seq, width, lengths, q, k, v, ck, cv):
    tokens, slots = q.shape[0], ck.shape[0]
    kv = jax.ShapeDtypeStruct((2 * tokens + 2 * slots + 16, width), jnp.bfloat16)
    qs = jax.ShapeDtypeStruct((tokens, width), jnp.bfloat16)
    anywhere = pl.BlockSpec(memory_space=pl.ANY)
    return pl.pallas_call(
        functools.partial(pack_kernel, seq, width, tokens, slots),
        out_shape=(kv, qs) * GROUPS,
        in_specs=[pl.BlockSpec(memory_space=pltpu.SMEM)] + [anywhere] * 5,
        out_specs=[anywhere] * (2 * GROUPS),
        scratch_shapes=[
            pltpu.VMEM((16, width), jnp.bfloat16),
            pltpu.SemaphoreType.DMA((6 * GROUPS,)),
        ],
        name="pack",
    )(lengths, q, k, v, ck, cv)


def attend_kernel(n_kv, n_q, tokens, slots, *refs):
    kvs, qs = refs[:n_kv], refs[n_kv : n_kv + n_q]
    outs = refs[n_kv + n_q : n_kv + 2 * n_q]
    keys, values, flags, sems = refs[n_kv + 2 * n_q :]
    block = n_kv * tokens
    copies = []
    for i, kv in enumerate(kvs):
        copies.append((kv.at[pl.ds(0, tokens), :], keys.at[pl.ds(i * tokens, tokens), :]))
        copies.append((kv.at[pl.ds(tokens, tokens), :], values.at[pl.ds(i * tokens, tokens), :]))
        copies.append((kv.at[pl.ds(2 * tokens, slots), :], keys.at[pl.ds(block + i * slots, slots), :]))
        copies.append(
            (kv.at[pl.ds(2 * tokens + slots, slots), :], values.at[pl.ds(block + i * slots, slots), :])
        )
        copies.append((kv.at[pl.ds(2 * tokens + 2 * slots, 16), pl.ds(0, 128)], flags.at[i]))
    run_copies(copies, sems)
    cached = n_kv * slots
    lane = lax.broadcasted_iota(jnp.int32, (1, 128), 1)
    each = 128 // slots
    pieces = []
    for start in range(0, n_kv, each):
        row = jnp.zeros((1, 128), jnp.float32)
        for j in range(each):
            flag = flags[start + j, 0:1, :].astype(jnp.float32)
            row = jnp.where(lax.div(lane, slots) == j, flag, row)
        pieces.append(row)
    usable = jnp.concatenate(pieces, axis=1) > 0.5
    scale = math.log2(math.e) / math.sqrt(DH)
    heads = keys.shape[1] // DH
    for h in range(heads):
        cols = slice(h * DH, (h + 1) * DH)
        for j in range(n_q):
            query = qs[j][:, cols]
            contract = (((1,), (1,)), ((), ()))
            main = lax.dot_general(
                query, keys[0:block, cols], contract, preferred_element_type=jnp.float32
            )
            tail = lax.dot_general(
                query, keys[block : block + cached, cols], contract, preferred_element_type=jnp.float32
            )
            tail = jnp.where(usable, tail, -3e38)
            top = jnp.maximum(
                jnp.max(main, axis=1, keepdims=True), jnp.max(tail, axis=1, keepdims=True)
            )
            main = jnp.exp2((main - top) * scale)
            tail = jnp.exp2((tail - top) * scale)
            total = jnp.sum(main, axis=1, keepdims=True) + jnp.sum(tail, axis=1, keepdims=True)
            mixed = jnp.dot(
                main.astype(jnp.bfloat16), values[0:block, cols], preferred_element_type=jnp.float32
            ) + jnp.dot(
                tail.astype(jnp.bfloat16),
                values[block : block + cached, cols],
                preferred_element_type=jnp.float32,
            )
            outs[j][:, cols] = (mixed / total).astype(jnp.bfloat16)


def attend(kvs, qs, tokens, slots):
    width = qs[0].shape[1]
    rows = len(kvs) * (tokens + slots)
    return pl.pallas_call(
        functools.partial(attend_kernel, len(kvs), len(qs), tokens, slots),
        out_shape=[jax.ShapeDtypeStruct((tokens, width), jnp.bfloat16)] * len(qs),
        in_specs=[pl.BlockSpec(memory_space=pl.ANY)] * len(kvs)
        + [pl.BlockSpec(memory_space=pltpu.VMEM)] * len(qs),
        out_specs=[pl.BlockSpec(memory_space=pltpu.VMEM)] * len(qs),
        scratch_shapes=[
            pltpu.VMEM((rows, width), jnp.bfloat16),
            pltpu.VMEM((rows, width), jnp.bfloat16),
            pltpu.VMEM((len(kvs), 16, 128), jnp.bfloat16),
            pltpu.SemaphoreType.DMA((5 * len(kvs),)),
        ],
        name="attend",
    )(*kvs, *qs)


def project_kernel(seq, other, n_parts, *refs):
    parts, w = refs[:n_parts], refs[n_parts]
    extra = refs[n_parts + 1 : -3]
    out, wbuf, sems = refs[-3:]
    me = lax.div(lax.axis_index("seq"), seq // GROUPS)
    x = lax.axis_index("head")
    half = lax.bitwise_xor(x, 1) if other else x
    width, n = parts[0].shape[1], out.shape[1]
    cols = pl.ds(pl.multiple_of(half * n, n), n)
    copies = []
    for j in range(n_parts):
        rows = pl.ds(pl.multiple_of(lax.bitwise_xor(me, j) * width, width), width)
        copies.append(pltpu.make_async_copy(w.at[rows, cols], wbuf.at[j], sems.at[j]))
    for copy in copies:
        copy.start()
    acc = None
    for j in range(n_parts):
        copies[j].wait()
        term = jnp.dot(parts[j][...], wbuf[j], preferred_element_type=jnp.float32)
        acc = term if acc is None else acc + term
    for e in extra:
        acc = acc + e[...].astype(jnp.float32)
    out[...] = acc.astype(out.dtype)


def project(seq, other, parts, w, extra, dtype):
    tokens, width = parts[0].shape
    n = w.shape[1] // 2
    inside = pl.BlockSpec(memory_space=pltpu.VMEM)
    return pl.pallas_call(
        functools.partial(project_kernel, seq, other, len(parts)),
        out_shape=jax.ShapeDtypeStruct((tokens, n), dtype),
        in_specs=[inside] * len(parts)
        + [pl.BlockSpec(memory_space=pl.ANY)]
        + [inside] * len(extra),
        out_specs=inside,
        scratch_shapes=[
            pltpu.VMEM((len(parts), width, n), jnp.bfloat16),
            pltpu.SemaphoreType.DMA((len(parts),)),
        ],
        name="project_other" if other else "project_own",
    )(*parts, w, *extra)


def dealt_plan(
    seq, queries, block_keys, block_values, cache_keys, cache_values, cache_lengths, out_weight
):
    tokens, slots = queries.shape[0], cache_keys.shape[0]
    width = queries.shape[1] // GROUPS
    stride = seq // GROUPS
    rows_y = stride // CORES

    def over_z(x, step):
        return lax.ppermute(x, "seq", [(s, s ^ (step * stride)) for s in range(seq)])

    def over_y(x, step):
        return lax.ppermute(x, "seq", [(s, s ^ (step * CORES)) for s in range(seq)])

    def over_core(x):
        return lax.ppermute(x, "seq", [(s, s ^ 1) for s in range(seq)])

    packed = pack(
        seq, width, cache_lengths, queries, block_keys, block_values, cache_keys, cache_values
    )
    kvs = [packed[0]] + [over_z(packed[2 * j], j) for j in range(1, GROUPS)]
    qs = [packed[1]] + [over_z(packed[2 * j + 1], j) for j in range(1, GROUPS)]
    gathered = []
    for kv in kvs:
        near = [kv] + [over_y(kv, j) for j in range(1, rows_y)]
        for piece in near:
            gathered += [piece, over_core(piece)]
    mixed = attend(gathered, qs, tokens, slots)
    parts = [mixed[0]] + [over_z(mixed[j], j) for j in range(1, GROUPS)]
    theirs = project(seq, True, parts, out_weight, (), jnp.bfloat16)
    arrived = lax.ppermute(theirs, "head", [(0, 1), (1, 0)])
    own = project(seq, False, parts, out_weight, (), jnp.float32)
    return (own + arrived.astype(jnp.float32)).astype(jnp.bfloat16)


def on_device(seq, head, *args):
    queries, cache_keys = args[0], args[3]
    heads_here = queries.shape[1] // DH
    slots = cache_keys.shape[0]
    rows_y = seq // (GROUPS * CORES)
    fits = (
        head == 2
        and seq % (GROUPS * CORES) == 0
        and rows_y & (rows_y - 1) == 0
        and heads_here % GROUPS == 0
        and slots == 16
        and (seq * slots) % 128 == 0
        and queries.shape[0] % 16 == 0
        and args[6].shape[1] % 256 == 0
    )
    return dealt_plan(seq, *args) if fits else gathered_plan(*args)


def solution(mesh):
    return jax.shard_map(
        functools.partial(on_device, mesh.shape["seq"], mesh.shape["head"]),
        mesh=mesh,
        in_specs=(
            P("seq", "head"),
            P("seq", "head"),
            P("seq", "head"),
            P("seq", "head"),
            P("seq", "head"),
            P("seq"),
            P("head", None),
        ),
        out_specs=P("seq", "head"),
        check_vma=False,
    )
```

```python
import functools
import math

import jax
import jax.numpy as jnp
from jax import lax
from jax.experimental import pallas as pl
from jax.experimental.pallas import tpu as pltpu
from jax.sharding import PartitionSpec as P

DH = 128
NEG_BIG = -1e30
CORES = 2
GROUPS = 4


def fold_keys(running, query_heads, key_rows, value_rows, usable):
    maxima, totals, accumulated = running
    heads_here = query_heads.shape[1]
    head_width = query_heads.shape[2]
    key_heads = key_rows.reshape(key_rows.shape[0], heads_here, head_width)
    value_heads = value_rows.reshape(value_rows.shape[0], heads_here, head_width)
    scores = jnp.einsum(
        "qhd,khd->hqk", query_heads, key_heads, preferred_element_type=jnp.float32
    ) * (1.0 / math.sqrt(head_width))
    if usable is not None:
        scores = jnp.where(usable[None, None, :], scores, NEG_BIG)
    newest = jnp.maximum(maxima, jnp.max(scores, axis=2))
    carried = jnp.exp(maxima - newest)
    weights = jnp.exp(scores - newest[:, :, None])
    totals = totals * carried + jnp.sum(weights, axis=2)
    mixed = jnp.einsum(
        "hqk,khd->hqd",
        weights.astype(jnp.bfloat16),
        value_heads,
        preferred_element_type=jnp.float32,
    )
    accumulated = accumulated * carried[:, :, None] + mixed
    return (newest, totals, accumulated)


def cache_usable(lengths_piece, slots, row_count):
    slot_index = jnp.arange(row_count, dtype=jnp.int32) % slots
    slot_limit = jnp.repeat(lengths_piece.astype(jnp.int32), slots, total_repeat_length=row_count)
    return slot_index < slot_limit


def gathered_plan(
    queries, block_keys, block_values, cache_keys, cache_values, cache_lengths, out_weight
):
    tokens_here = queries.shape[0]
    heads_here = queries.shape[1] // DH
    query_heads = queries.reshape(tokens_here, heads_here, DH)
    slots = cache_keys.shape[0]
    running = (
        jnp.full((heads_here, tokens_here), NEG_BIG, jnp.float32),
        jnp.zeros((heads_here, tokens_here), jnp.float32),
        jnp.zeros((heads_here, tokens_here, DH), jnp.float32),
    )
    gather = functools.partial(lax.all_gather, axis_name="seq", axis=0, tiled=True)
    running = fold_keys(running, query_heads, gather(block_keys), gather(block_values), None)
    cached = gather(cache_keys)
    usable = cache_usable(gather(cache_lengths), slots, cached.shape[0])
    running = fold_keys(running, query_heads, cached, gather(cache_values), usable)
    _, totals, accumulated = running
    attended = (
        (accumulated / totals[:, :, None])
        .transpose(1, 0, 2)
        .reshape(tokens_here, heads_here * DH)
        .astype(jnp.bfloat16)
    )
    partial_terms = jnp.dot(attended, out_weight, preferred_element_type=jnp.float32)
    return lax.psum_scatter(
        partial_terms.astype(jnp.bfloat16), "head", scatter_dimension=1, tiled=True
    )


def inside():
    return pl.BlockSpec(memory_space=pltpu.VMEM)


def outside():
    return pl.BlockSpec(memory_space=pltpu.HBM)


def pack_kernel(seq, width, slots, len_ref, q, k, v, ck, cv, *refs):
    outs, sems = refs[: 2 * GROUPS], refs[2 * GROUPS]
    me = lax.div(lax.axis_index("seq"), seq // GROUPS)
    copies = []
    for step in (1, 2, 3, 0):
        group = lax.bitwise_xor(me, step)
        cols = pl.ds(pl.multiple_of(group * width, width), width)
        kv, qo = outs[2 * step], outs[2 * step + 1]
        row = 0
        for src in (k, v, ck, cv):
            rows = src.shape[0]
            copies.append((src.at[:, cols], kv.at[pl.ds(row, rows), :]))
            row += rows
        copies.append((q.at[:, cols], qo))
    started = [
        pltpu.make_async_copy(src, dst, sems.at[i]) for i, (src, dst) in enumerate(copies)
    ]
    for copy in started:
        copy.start()
    lane = lax.broadcasted_iota(jnp.int32, (16, width), 1)
    flags = jnp.where(lax.rem(lane, slots) < len_ref[0], 1.0, 0.0).astype(jnp.bfloat16)
    for step in range(GROUPS):
        kv = outs[2 * step]
        kv[kv.shape[0] - 16 :, :] = flags
    for copy in started:
        copy.wait()


def pack(seq, width, lengths, q, k, v, ck, cv):
    tokens, slots = q.shape[0], ck.shape[0]
    kv = jax.ShapeDtypeStruct((2 * tokens + 2 * slots + 16, width), jnp.bfloat16)
    qs = jax.ShapeDtypeStruct((tokens, width), jnp.bfloat16)
    return pl.pallas_call(
        functools.partial(pack_kernel, seq, width, slots),
        out_shape=(kv, qs) * GROUPS,
        in_specs=[pl.BlockSpec(memory_space=pltpu.SMEM)] + [outside()] * 5,
        out_specs=[inside()] * (2 * GROUPS),
        scratch_shapes=[pltpu.SemaphoreType.DMA((5 * GROUPS,))],
        compiler_params=pltpu.CompilerParams(vmem_limit_bytes=4 << 20),
        name="pack",
    )(lengths, q, k, v, ck, cv)


def gather_kernel(n_kv, tokens, slots, *refs):
    kvs, (keys, values, usable) = refs[:n_kv], refs[n_kv:]
    block = n_kv * tokens
    for i, kv in enumerate(kvs):
        keys[i * tokens : (i + 1) * tokens, :] = kv[0:tokens, :]
        values[i * tokens : (i + 1) * tokens, :] = kv[tokens : 2 * tokens, :]
        at = slice(block + i * slots, block + (i + 1) * slots)
        keys[at, :] = kv[2 * tokens : 2 * tokens + slots, :]
        values[at, :] = kv[2 * tokens + slots : 2 * tokens + 2 * slots, :]
    lane = lax.broadcasted_iota(jnp.int32, (16, 128), 1)
    each = 128 // slots
    for start in range(0, n_kv, each):
        row = jnp.zeros((16, 128), jnp.float32)
        for j in range(each):
            kv = kvs[start + j]
            flag = kv[kv.shape[0] - 16 :, 0:128].astype(jnp.float32)
            row = jnp.where(lax.div(lane, slots) == j, flag, row)
        usable[:, start * slots : start * slots + 128] = row


def attend_rows(keys, values, usable, query, block, cols):
    scale = math.log2(math.e) / math.sqrt(DH)
    contract = (((1,), (1,)), ((), ()))
    main = lax.dot_general(
        query, keys[0:block, cols], contract, preferred_element_type=jnp.float32
    )
    tail = lax.dot_general(
        query, keys[block:, cols], contract, preferred_element_type=jnp.float32
    )
    tail = jnp.where(usable, tail, -3e38)
    top = jnp.maximum(jnp.max(main, axis=1, keepdims=True), jnp.max(tail, axis=1, keepdims=True))
    main = jnp.exp2((main - top) * scale)
    tail = jnp.exp2((tail - top) * scale)
    total = jnp.sum(main, axis=1, keepdims=True) + jnp.sum(tail, axis=1, keepdims=True)
    mixed = jnp.dot(
        main.astype(jnp.bfloat16), values[0:block, cols], preferred_element_type=jnp.float32
    ) + jnp.dot(tail.astype(jnp.bfloat16), values[block:, cols], preferred_element_type=jnp.float32)
    return (mixed / total).astype(jnp.bfloat16)


def attend_kernel(block, n_q, *refs):
    keys, values, usable = refs[:3]
    qs, outs = refs[3 : 3 + n_q], refs[3 + n_q : 3 + 2 * n_q]
    query = refs[3 + 2 * n_q]
    tokens = qs[0].shape[0]
    flags = usable[0:1, :] > 0.5
    for j in range(n_q):
        query[j * tokens : (j + 1) * tokens, :] = qs[j][...]
    for h in range(keys.shape[1] // DH):
        cols = slice(h * DH, (h + 1) * DH)
        out = attend_rows(keys, values, flags, query[:, cols], block, cols)
        for j in range(n_q):
            outs[j][:, cols] = out[j * tokens : (j + 1) * tokens]


def gather_and_attend_kernel(n_kv, n_q, tokens, slots, *refs):
    kvs, qs = refs[:n_kv], refs[n_kv : n_kv + n_q]
    outs = refs[n_kv + n_q : n_kv + 2 * n_q]
    whole, query = refs[n_kv + 2 * n_q : -1], refs[-1]
    gather_kernel(n_kv, tokens, slots, *kvs, *whole)
    attend_kernel(n_kv * tokens, n_q, *whole, *qs, *outs, query)


def gather_and_attend(kvs, qs, slots):
    tokens, width = qs[0].shape
    rows = len(kvs) * (tokens + slots)
    out = jax.ShapeDtypeStruct((tokens, width), jnp.bfloat16)
    rows_kept = jax.ShapeDtypeStruct((rows, width), jnp.bfloat16)
    flags = jax.ShapeDtypeStruct((16, len(kvs) * slots), jnp.float32)
    made = pl.pallas_call(
        functools.partial(gather_and_attend_kernel, len(kvs), len(qs), tokens, slots),
        out_shape=[out] * len(qs) + [rows_kept, rows_kept, flags],
        in_specs=[inside()] * (len(kvs) + len(qs)),
        out_specs=[inside()] * (len(qs) + 3),
        scratch_shapes=[pltpu.VMEM((len(qs) * tokens, width), jnp.bfloat16)],
        compiler_params=pltpu.CompilerParams(vmem_limit_bytes=24 << 20),
        name="gather_and_attend",
    )(*kvs, *qs)
    return made[: len(qs)], made[len(qs) :]


def attend(kept, qs, block):
    tokens, width = qs[0].shape
    return pl.pallas_call(
        functools.partial(attend_kernel, block, len(qs)),
        out_shape=[jax.ShapeDtypeStruct((tokens, width), jnp.bfloat16)] * len(qs),
        in_specs=[inside()] * (3 + len(qs)),
        out_specs=[inside()] * len(qs),
        scratch_shapes=[pltpu.VMEM((len(qs) * tokens, width), jnp.bfloat16)],
        compiler_params=pltpu.CompilerParams(vmem_limit_bytes=16 << 20),
        name="attend",
    )(*kept, *qs)


def stage_kernel(seq, other, w, after, out, sems):
    del after
    me = lax.div(lax.axis_index("seq"), seq // GROUPS)
    x = lax.axis_index("head")
    half = lax.bitwise_xor(x, 1) if other else x
    width, n = out.shape[0] // GROUPS, out.shape[1]
    cols = pl.ds(pl.multiple_of(half * n, n), n)
    copies = []
    for j in range(GROUPS):
        rows = pl.ds(pl.multiple_of(lax.bitwise_xor(me, j) * width, width), width)
        copies.append(
            pltpu.make_async_copy(w.at[rows, cols], out.at[pl.ds(j * width, width), :], sems.at[j])
        )
    for copy in copies:
        copy.start()
    for copy in copies:
        copy.wait()


def stage(seq, other, w, after):
    return pl.pallas_call(
        functools.partial(stage_kernel, seq, other),
        out_shape=jax.ShapeDtypeStruct((w.shape[0], w.shape[1] // 2), w.dtype),
        in_specs=[outside(), outside()],
        out_specs=inside(),
        scratch_shapes=[pltpu.SemaphoreType.DMA((GROUPS,))],
        compiler_params=pltpu.CompilerParams(vmem_limit_bytes=45 << 20),
        name="stage_other" if other else "stage_own",
    )(w, after)


def project_kernel(start, n_parts, *refs):
    parts, w, out = refs[:n_parts], refs[n_parts], refs[n_parts + 1]
    n = out.shape[1]
    attended = jnp.concatenate([p[...] for p in parts], axis=1)
    out[...] = jnp.dot(
        attended, w[:, start : start + n], preferred_element_type=jnp.float32
    ).astype(out.dtype)


def project(parts, w, start, n, dtype):
    return pl.pallas_call(
        functools.partial(project_kernel, start, len(parts)),
        out_shape=jax.ShapeDtypeStruct((parts[0].shape[0], n), dtype),
        in_specs=[inside()] * (len(parts) + 1),
        out_specs=inside(),
        compiler_params=pltpu.CompilerParams(vmem_limit_bytes=8 << 20),
        name="project",
    )(*parts, w)


def add_kernel(own, *refs):
    out, start = refs[-1], 0
    for piece in refs[:-1]:
        n = piece.shape[1]
        at = slice(start, start + n)
        out[:, at] = (own[:, at] + piece[...].astype(jnp.float32)).astype(out.dtype)
        start += n


def add(own, pieces):
    return pl.pallas_call(
        add_kernel,
        out_shape=jax.ShapeDtypeStruct(own.shape, jnp.bfloat16),
        in_specs=[inside()] * (1 + len(pieces)),
        out_specs=inside(),
        compiler_params=pltpu.CompilerParams(vmem_limit_bytes=4 << 20),
        name="add",
    )(own, *pieces)


def dealt_plan(
    seq, queries, block_keys, block_values, cache_keys, cache_values, cache_lengths, out_weight
):
    tokens, slots = queries.shape[0], cache_keys.shape[0]
    width = queries.shape[1] // GROUPS
    stride = seq // GROUPS
    rows_y = stride // CORES

    def over(x, flip):
        return lax.ppermute(x, "seq", [(s, s ^ flip) for s in range(seq)])

    def over_z(x, step):
        return over(x, step * stride)

    def over_y(x, step):
        return over(x, step * CORES)

    packed = pack(
        seq, width, cache_lengths, queries, block_keys, block_values, cache_keys, cache_values
    )
    kvs = [packed[0]] + [over_z(packed[2 * j], j) for j in range(1, GROUPS)]
    qs = [packed[1]] + [over_z(packed[2 * j + 1], j) for j in range(1, GROUPS)]
    gathered = []
    for kv in kvs:
        near = [kv] + [over_y(kv, j) for j in range(1, rows_y)]
        for piece in near:
            gathered += [piece, over(piece, 1)]
    late, kept = gather_and_attend(gathered, qs[2:], slots)
    early = attend(kept, qs[:2], len(gathered) * tokens)
    parts = [early[0], over_z(early[1], 1), over_z(late[0], 2), over_z(late[1], 3)]
    w_other = stage(seq, True, out_weight, packed[1])
    w_own = stage(seq, False, out_weight, packed[1])
    half = w_own.shape[1]
    cuts = [0, half // 4, half]
    arrived = []
    for i in range(len(cuts) - 1):
        theirs = project(parts, w_other, cuts[i], cuts[i + 1] - cuts[i], jnp.bfloat16)
        arrived.append(lax.ppermute(theirs, "head", [(0, 1), (1, 0)]))
    own = project(parts, w_own, 0, half, jnp.float32)
    return add(own, arrived)


def on_device(seq, head, *args):
    queries, cache_keys = args[0], args[3]
    heads_here = queries.shape[1] // DH
    slots = cache_keys.shape[0]
    rows_y = seq // (GROUPS * CORES)
    fits = (
        head == 2
        and seq % (GROUPS * CORES) == 0
        and rows_y & (rows_y - 1) == 0
        and heads_here % GROUPS == 0
        and slots == 16
        and (seq * slots) % 128 == 0
        and queries.shape[0] % 16 == 0
        and args[6].shape[1] % 1024 == 0
    )
    return dealt_plan(seq, *args) if fits else gathered_plan(*args)


def solution(mesh):
    return jax.shard_map(
        functools.partial(on_device, mesh.shape["seq"], mesh.shape["head"]),
        mesh=mesh,
        in_specs=(
            P("seq", "head"),
            P("seq", "head"),
            P("seq", "head"),
            P("seq", "head"),
            P("seq", "head"),
            P("seq"),
            P("head", None),
        ),
        out_specs=P("seq", "head"),
        check_vma=False,
    )
```

```python
import functools
import math

import jax
import jax.numpy as jnp
from jax import lax
from jax.experimental import pallas as pl
from jax.experimental.pallas import tpu as pltpu
from jax.sharding import PartitionSpec as P

DH = 128
NEG_BIG = -1e30
CORES = 2
GROUPS = 4


def fold_keys(running, query_heads, key_rows, value_rows, usable):
    maxima, totals, accumulated = running
    heads_here = query_heads.shape[1]
    head_width = query_heads.shape[2]
    key_heads = key_rows.reshape(key_rows.shape[0], heads_here, head_width)
    value_heads = value_rows.reshape(value_rows.shape[0], heads_here, head_width)
    scores = jnp.einsum(
        "qhd,khd->hqk", query_heads, key_heads, preferred_element_type=jnp.float32
    ) * (1.0 / math.sqrt(head_width))
    if usable is not None:
        scores = jnp.where(usable[None, None, :], scores, NEG_BIG)
    newest = jnp.maximum(maxima, jnp.max(scores, axis=2))
    carried = jnp.exp(maxima - newest)
    weights = jnp.exp(scores - newest[:, :, None])
    totals = totals * carried + jnp.sum(weights, axis=2)
    mixed = jnp.einsum(
        "hqk,khd->hqd",
        weights.astype(jnp.bfloat16),
        value_heads,
        preferred_element_type=jnp.float32,
    )
    accumulated = accumulated * carried[:, :, None] + mixed
    return (newest, totals, accumulated)


def cache_usable(lengths_piece, slots, row_count):
    slot_index = jnp.arange(row_count, dtype=jnp.int32) % slots
    slot_limit = jnp.repeat(lengths_piece.astype(jnp.int32), slots, total_repeat_length=row_count)
    return slot_index < slot_limit


def gathered_plan(
    queries, block_keys, block_values, cache_keys, cache_values, cache_lengths, out_weight
):
    tokens_here = queries.shape[0]
    heads_here = queries.shape[1] // DH
    query_heads = queries.reshape(tokens_here, heads_here, DH)
    slots = cache_keys.shape[0]
    running = (
        jnp.full((heads_here, tokens_here), NEG_BIG, jnp.float32),
        jnp.zeros((heads_here, tokens_here), jnp.float32),
        jnp.zeros((heads_here, tokens_here, DH), jnp.float32),
    )
    gather = functools.partial(lax.all_gather, axis_name="seq", axis=0, tiled=True)
    running = fold_keys(running, query_heads, gather(block_keys), gather(block_values), None)
    cached = gather(cache_keys)
    usable = cache_usable(gather(cache_lengths), slots, cached.shape[0])
    running = fold_keys(running, query_heads, cached, gather(cache_values), usable)
    _, totals, accumulated = running
    attended = (
        (accumulated / totals[:, :, None])
        .transpose(1, 0, 2)
        .reshape(tokens_here, heads_here * DH)
        .astype(jnp.bfloat16)
    )
    partial_terms = jnp.dot(attended, out_weight, preferred_element_type=jnp.float32)
    return lax.psum_scatter(
        partial_terms.astype(jnp.bfloat16), "head", scatter_dimension=1, tiled=True
    )


def inside():
    return pl.BlockSpec(memory_space=pltpu.VMEM)


def outside():
    return pl.BlockSpec(memory_space=pltpu.HBM)


def pack_kernel(seq, width, slots, len_ref, q, k, v, ck, cv, *refs):
    outs, sems = refs[: 2 * GROUPS], refs[2 * GROUPS]
    me = lax.div(lax.axis_index("seq"), seq // GROUPS)
    copies = []
    for step in (1, 2, 3, 0):
        group = lax.bitwise_xor(me, step)
        cols = pl.ds(pl.multiple_of(group * width, width), width)
        kv, qo = outs[2 * step], outs[2 * step + 1]
        row = 0
        for src in (k, v, ck, cv):
            rows = src.shape[0]
            copies.append((src.at[:, cols], kv.at[pl.ds(row, rows), :]))
            row += rows
        copies.append((q.at[:, cols], qo))
    started = [
        pltpu.make_async_copy(src, dst, sems.at[i]) for i, (src, dst) in enumerate(copies)
    ]
    for copy in started:
        copy.start()
    lane = lax.broadcasted_iota(jnp.int32, (16, width), 1)
    flags = jnp.where(lax.rem(lane, slots) < len_ref[0], 1.0, 0.0).astype(jnp.bfloat16)
    for step in range(GROUPS):
        kv = outs[2 * step]
        kv[kv.shape[0] - 16 :, :] = flags
    for copy in started:
        copy.wait()


def pack(seq, width, lengths, q, k, v, ck, cv):
    tokens, slots = q.shape[0], ck.shape[0]
    kv = jax.ShapeDtypeStruct((2 * tokens + 2 * slots + 16, width), jnp.bfloat16)
    qs = jax.ShapeDtypeStruct((tokens, width), jnp.bfloat16)
    return pl.pallas_call(
        functools.partial(pack_kernel, seq, width, slots),
        out_shape=(kv, qs) * GROUPS,
        in_specs=[pl.BlockSpec(memory_space=pltpu.SMEM)] + [outside()] * 5,
        out_specs=[inside()] * (2 * GROUPS),
        scratch_shapes=[pltpu.SemaphoreType.DMA((5 * GROUPS,))],
        compiler_params=pltpu.CompilerParams(vmem_limit_bytes=61 << 20),
        name="pack",
    )(lengths, q, k, v, ck, cv)


def hold_kernel(*refs):
    for src, dst in zip(refs[: len(refs) // 2], refs[len(refs) // 2 :]):
        dst[...] = src[...]


def hold(*arrays):
    return pl.pallas_call(
        hold_kernel,
        out_shape=[jax.ShapeDtypeStruct(a.shape, a.dtype) for a in arrays],
        in_specs=[inside()] * len(arrays),
        out_specs=[inside()] * len(arrays),
        compiler_params=pltpu.CompilerParams(vmem_limit_bytes=4 << 20),
        name="hold",
    )(*arrays)


def gather_kernel(n_kv, tokens, slots, *refs):
    kvs, (keys, values, usable) = refs[:n_kv], refs[n_kv:]
    block = n_kv * tokens
    for i, kv in enumerate(kvs):
        keys[i * tokens : (i + 1) * tokens, :] = kv[0:tokens, :]
        values[i * tokens : (i + 1) * tokens, :] = kv[tokens : 2 * tokens, :]
        at = slice(block + i * slots, block + (i + 1) * slots)
        keys[at, :] = kv[2 * tokens : 2 * tokens + slots, :]
        values[at, :] = kv[2 * tokens + slots : 2 * tokens + 2 * slots, :]
    lane = lax.broadcasted_iota(jnp.int32, (16, 128), 1)
    each = 128 // slots
    for start in range(0, n_kv, each):
        row = jnp.zeros((16, 128), jnp.float32)
        for j in range(each):
            kv = kvs[start + j]
            flag = kv[kv.shape[0] - 16 :, 0:128].astype(jnp.float32)
            row = jnp.where(lax.div(lane, slots) == j, flag, row)
        usable[:, start * slots : start * slots + 128] = row


def attend_rows(keys, values, usable, query, block, cols):
    scale = math.log2(math.e) / math.sqrt(DH)
    contract = (((1,), (1,)), ((), ()))
    main = lax.dot_general(
        query, keys[0:block, cols], contract, preferred_element_type=jnp.float32
    )
    tail = lax.dot_general(
        query, keys[block:, cols], contract, preferred_element_type=jnp.float32
    )
    tail = jnp.where(usable, tail, -3e38)
    top = jnp.maximum(jnp.max(main, axis=1, keepdims=True), jnp.max(tail, axis=1, keepdims=True))
    main = jnp.exp2((main - top) * scale)
    tail = jnp.exp2((tail - top) * scale)
    total = jnp.sum(main, axis=1, keepdims=True) + jnp.sum(tail, axis=1, keepdims=True)
    mixed = jnp.dot(
        main.astype(jnp.bfloat16), values[0:block, cols], preferred_element_type=jnp.float32
    ) + jnp.dot(tail.astype(jnp.bfloat16), values[block:, cols], preferred_element_type=jnp.float32)
    return (mixed / total).astype(jnp.bfloat16)


def attend_kernel(block, n_q, *refs):
    keys, values, usable = refs[:3]
    qs, outs = refs[3 : 3 + n_q], refs[3 + n_q : 3 + 2 * n_q]
    query = refs[3 + 2 * n_q]
    tokens = qs[0].shape[0]
    flags = usable[0:1, :] > 0.5
    for j in range(n_q):
        query[j * tokens : (j + 1) * tokens, :] = qs[j][...]
    for h in range(keys.shape[1] // DH):
        cols = slice(h * DH, (h + 1) * DH)
        out = attend_rows(keys, values, flags, query[:, cols], block, cols)
        for j in range(n_q):
            outs[j][:, cols] = out[j * tokens : (j + 1) * tokens]


def gather_and_attend_kernel(n_kv, n_q, tokens, slots, *refs):
    kvs, qs = refs[:n_kv], refs[n_kv : n_kv + n_q]
    outs = refs[n_kv + n_q : n_kv + 2 * n_q]
    whole, query = refs[n_kv + 2 * n_q : -1], refs[-1]
    gather_kernel(n_kv, tokens, slots, *kvs, *whole)
    attend_kernel(n_kv * tokens, n_q, *whole, *qs, *outs, query)


def gather_and_attend(kvs, qs, slots):
    tokens, width = qs[0].shape
    rows = len(kvs) * (tokens + slots)
    out = jax.ShapeDtypeStruct((tokens, width), jnp.bfloat16)
    rows_kept = jax.ShapeDtypeStruct((rows, width), jnp.bfloat16)
    flags = jax.ShapeDtypeStruct((16, len(kvs) * slots), jnp.float32)
    made = pl.pallas_call(
        functools.partial(gather_and_attend_kernel, len(kvs), len(qs), tokens, slots),
        out_shape=[out] * len(qs) + [rows_kept, rows_kept, flags],
        in_specs=[inside()] * (len(kvs) + len(qs)),
        out_specs=[inside()] * (len(qs) + 3),
        scratch_shapes=[pltpu.VMEM((len(qs) * tokens, width), jnp.bfloat16)],
        compiler_params=pltpu.CompilerParams(vmem_limit_bytes=24 << 20),
        name="gather_and_attend",
    )(*kvs, *qs)
    return made[: len(qs)], made[len(qs) :]


def attend(kept, qs, block):
    tokens, width = qs[0].shape
    return pl.pallas_call(
        functools.partial(attend_kernel, block, len(qs)),
        out_shape=[jax.ShapeDtypeStruct((tokens, width), jnp.bfloat16)] * len(qs),
        in_specs=[inside()] * (3 + len(qs)),
        out_specs=[inside()] * len(qs),
        scratch_shapes=[pltpu.VMEM((len(qs) * tokens, width), jnp.bfloat16)],
        compiler_params=pltpu.CompilerParams(vmem_limit_bytes=16 << 20),
        name="attend",
    )(*kept, *qs)


def stage_kernel(seq, other, w, out, sems):
    me = lax.div(lax.axis_index("seq"), seq // GROUPS)
    x = lax.axis_index("head")
    half = lax.bitwise_xor(x, 1) if other else x
    width, n = out.shape[0] // GROUPS, out.shape[1]
    cols = pl.ds(pl.multiple_of(half * n, n), n)
    copies = []
    for j in range(GROUPS):
        rows = pl.ds(pl.multiple_of(lax.bitwise_xor(me, j) * width, width), width)
        copies.append(
            pltpu.make_async_copy(w.at[rows, cols], out.at[pl.ds(j * width, width), :], sems.at[j])
        )
    for copy in copies:
        copy.start()
    for copy in copies:
        copy.wait()


def stage(seq, other, w):
    return pl.pallas_call(
        functools.partial(stage_kernel, seq, other),
        out_shape=jax.ShapeDtypeStruct((w.shape[0], w.shape[1] // 2), w.dtype),
        in_specs=[outside()],
        out_specs=inside(),
        scratch_shapes=[pltpu.SemaphoreType.DMA((GROUPS,))],
        compiler_params=pltpu.CompilerParams(vmem_limit_bytes=45 << 20),
        name="stage_other" if other else "stage_own",
    )(w)


def project_kernel(start, n_parts, *refs):
    parts, w, out = refs[:n_parts], refs[n_parts], refs[n_parts + 1]
    n = out.shape[1]
    attended = jnp.concatenate([p[...] for p in parts], axis=1)
    out[...] = jnp.dot(
        attended, w[:, start : start + n], preferred_element_type=jnp.float32
    ).astype(out.dtype)


def project(parts, w, start, n, dtype):
    return pl.pallas_call(
        functools.partial(project_kernel, start, len(parts)),
        out_shape=jax.ShapeDtypeStruct((parts[0].shape[0], n), dtype),
        in_specs=[inside()] * (len(parts) + 1),
        out_specs=inside(),
        compiler_params=pltpu.CompilerParams(vmem_limit_bytes=8 << 20),
        name="project",
    )(*parts, w)


def add_kernel(own, *refs):
    out, start = refs[-1], 0
    for piece in refs[:-1]:
        n = piece.shape[1]
        at = slice(start, start + n)
        out[:, at] = (own[:, at] + piece[...].astype(jnp.float32)).astype(out.dtype)
        start += n


def add(own, pieces):
    return pl.pallas_call(
        add_kernel,
        out_shape=jax.ShapeDtypeStruct(own.shape, jnp.bfloat16),
        in_specs=[inside()] * (1 + len(pieces)),
        out_specs=inside(),
        compiler_params=pltpu.CompilerParams(vmem_limit_bytes=4 << 20),
        name="add",
    )(own, *pieces)


def dealt_plan(
    seq, queries, block_keys, block_values, cache_keys, cache_values, cache_lengths, out_weight
):
    tokens, slots = queries.shape[0], cache_keys.shape[0]
    width = queries.shape[1] // GROUPS
    stride = seq // GROUPS
    rows_y = stride // CORES

    def over(x, flip):
        return lax.ppermute(x, "seq", [(s, s ^ flip) for s in range(seq)])

    def over_z(x, step):
        return over(x, step * stride)

    def over_y(x, step):
        return over(x, step * CORES)

    packed = pack(
        seq, width, cache_lengths, queries, block_keys, block_values, cache_keys, cache_values
    )
    kvs = [packed[0]] + [over_z(packed[2 * j], j) for j in range(1, GROUPS)]
    qs = [packed[1]] + [over_z(packed[2 * j + 1], j) for j in range(1, GROUPS)]
    kept_kv, qs[0] = hold(kvs[0], qs[0])
    gathered = []
    for i, kv in enumerate(kvs):
        near = [kv] + [over_y(kv, j) for j in range(1, rows_y)]
        for j, piece in enumerate(near):
            kept = kept_kv if i == j == 0 else piece
            gathered += [kept, over(piece, 1)]
    late, kept = gather_and_attend(gathered, qs[2:], slots)
    early = attend(kept, qs[:2], len(gathered) * tokens)
    parts = [early[0], over_z(early[1], 1), over_z(late[0], 2), over_z(late[1], 3)]
    w_other = stage(seq, True, out_weight)
    w_own = stage(seq, False, out_weight)
    half = w_own.shape[1]
    cuts = [0, half // 4, half]
    arrived = []
    for i in range(len(cuts) - 1):
        theirs = project(parts, w_other, cuts[i], cuts[i + 1] - cuts[i], jnp.bfloat16)
        arrived.append(lax.ppermute(theirs, "head", [(0, 1), (1, 0)]))
    own = project(parts, w_own, 0, half, jnp.float32)
    return add(own, arrived)


def on_device(seq, head, *args):
    queries, cache_keys = args[0], args[3]
    heads_here = queries.shape[1] // DH
    slots = cache_keys.shape[0]
    rows_y = seq // (GROUPS * CORES)
    fits = (
        head == 2
        and seq % (GROUPS * CORES) == 0
        and rows_y & (rows_y - 1) == 0
        and heads_here % GROUPS == 0
        and slots == 16
        and (seq * slots) % 128 == 0
        and queries.shape[0] % 16 == 0
        and args[6].shape[1] % 1024 == 0
    )
    return dealt_plan(seq, *args) if fits else gathered_plan(*args)


def solution(mesh):
    return jax.shard_map(
        functools.partial(on_device, mesh.shape["seq"], mesh.shape["head"]),
        mesh=mesh,
        in_specs=(
            P("seq", "head"),
            P("seq", "head"),
            P("seq", "head"),
            P("seq", "head"),
            P("seq", "head"),
            P("seq"),
            P("head", None),
        ),
        out_specs=P("seq", "head"),
        check_vma=False,
    )
```

```python
import functools
import math

import jax
import jax.numpy as jnp
from jax import lax
from jax.experimental import pallas as pl
from jax.experimental.pallas import tpu as pltpu
from jax.sharding import PartitionSpec as P

DH = 128
NEG_BIG = -1e30
CORES = 2
GROUPS = 4


def fold_keys(running, query_heads, key_rows, value_rows, usable):
    maxima, totals, accumulated = running
    heads_here = query_heads.shape[1]
    head_width = query_heads.shape[2]
    key_heads = key_rows.reshape(key_rows.shape[0], heads_here, head_width)
    value_heads = value_rows.reshape(value_rows.shape[0], heads_here, head_width)
    scores = jnp.einsum(
        "qhd,khd->hqk", query_heads, key_heads, preferred_element_type=jnp.float32
    ) * (1.0 / math.sqrt(head_width))
    if usable is not None:
        scores = jnp.where(usable[None, None, :], scores, NEG_BIG)
    newest = jnp.maximum(maxima, jnp.max(scores, axis=2))
    carried = jnp.exp(maxima - newest)
    weights = jnp.exp(scores - newest[:, :, None])
    totals = totals * carried + jnp.sum(weights, axis=2)
    mixed = jnp.einsum(
        "hqk,khd->hqd",
        weights.astype(jnp.bfloat16),
        value_heads,
        preferred_element_type=jnp.float32,
    )
    accumulated = accumulated * carried[:, :, None] + mixed
    return (newest, totals, accumulated)


def cache_usable(lengths_piece, slots, row_count):
    slot_index = jnp.arange(row_count, dtype=jnp.int32) % slots
    slot_limit = jnp.repeat(lengths_piece.astype(jnp.int32), slots, total_repeat_length=row_count)
    return slot_index < slot_limit


def gathered_plan(
    queries, block_keys, block_values, cache_keys, cache_values, cache_lengths, out_weight
):
    tokens_here = queries.shape[0]
    heads_here = queries.shape[1] // DH
    query_heads = queries.reshape(tokens_here, heads_here, DH)
    slots = cache_keys.shape[0]
    running = (
        jnp.full((heads_here, tokens_here), NEG_BIG, jnp.float32),
        jnp.zeros((heads_here, tokens_here), jnp.float32),
        jnp.zeros((heads_here, tokens_here, DH), jnp.float32),
    )
    gather = functools.partial(lax.all_gather, axis_name="seq", axis=0, tiled=True)
    running = fold_keys(running, query_heads, gather(block_keys), gather(block_values), None)
    cached = gather(cache_keys)
    usable = cache_usable(gather(cache_lengths), slots, cached.shape[0])
    running = fold_keys(running, query_heads, cached, gather(cache_values), usable)
    _, totals, accumulated = running
    attended = (
        (accumulated / totals[:, :, None])
        .transpose(1, 0, 2)
        .reshape(tokens_here, heads_here * DH)
        .astype(jnp.bfloat16)
    )
    partial_terms = jnp.dot(attended, out_weight, preferred_element_type=jnp.float32)
    return lax.psum_scatter(
        partial_terms.astype(jnp.bfloat16), "head", scatter_dimension=1, tiled=True
    )


def inside():
    return pl.BlockSpec(memory_space=pltpu.VMEM)


def outside():
    return pl.BlockSpec(memory_space=pltpu.HBM)


def pack_kernel(seq, width, late, slots, len_ref, q, k, v, ck, cv, *refs):
    outs, sems = refs[:-1], refs[-1]
    own_kv, own_q = outs[:2]
    first, last = outs[2 : 2 * GROUPS], outs[2 * GROUPS :]
    me = lax.div(lax.axis_index("seq"), seq // GROUPS)
    copies = []

    def cut(kv, group, start, n):
        cols = pl.ds(pl.multiple_of(group * width + start, 128), n)
        row = 0
        for src in (k, v, ck, cv):
            rows = src.shape[0]
            copies.append((src.at[:, cols], kv.at[pl.ds(row, rows), :]))
            row += rows
        return cols

    for step in range(1, GROUPS):
        kv, qo = first[2 * step - 2], first[2 * step - 1]
        cols = cut(kv, lax.bitwise_xor(me, step), 0, width - late)
        copies.append((q.at[:, cols], qo))
    copies.append((q.at[:, cut(own_kv, me, 0, width)], own_q))
    for step in range(1, GROUPS):
        kv = last[step - 1]
        cols = cut(kv, lax.bitwise_xor(me, step), width - late, late)
        tokens = q.shape[0]
        copies.append((q.at[:, cols], kv.at[pl.ds(kv.shape[0] - tokens, tokens), :]))
    started = [
        pltpu.make_async_copy(src, dst, sems.at[i]) for i, (src, dst) in enumerate(copies)
    ]
    for copy in started:
        copy.start()
    row = 2 * k.shape[0] + 2 * slots
    for kv in (own_kv, *first[::2], *last):
        lane = lax.broadcasted_iota(jnp.int32, (16, kv.shape[1]), 1)
        kv[row : row + 16, :] = jnp.where(lax.rem(lane, slots) < len_ref[0], 1.0, 0.0).astype(
            jnp.bfloat16
        )
    for copy in started:
        copy.wait()


def pack(seq, width, late, lengths, q, k, v, ck, cv):
    tokens, slots = q.shape[0], ck.shape[0]
    rows = 2 * tokens + 2 * slots + 16

    def array(n, columns):
        return jax.ShapeDtypeStruct((n, columns), jnp.bfloat16)

    shapes = [array(rows, width), array(tokens, width)]
    shapes += [array(rows, width - late), array(tokens, width - late)] * (GROUPS - 1)
    shapes += [array(rows + tokens, late)] * (GROUPS - 1)
    made = pl.pallas_call(
        functools.partial(pack_kernel, seq, width, late, slots),
        out_shape=shapes,
        in_specs=[pl.BlockSpec(memory_space=pltpu.SMEM)] + [outside()] * 5,
        out_specs=[inside()] * len(shapes),
        scratch_shapes=[pltpu.SemaphoreType.DMA((5 * (2 * GROUPS - 1),))],
        compiler_params=pltpu.CompilerParams(vmem_limit_bytes=61 << 20),
        name="pack",
    )(lengths, q, k, v, ck, cv)
    return made[:2], made[2 : 2 * GROUPS], made[2 * GROUPS :]


def hold_kernel(*refs):
    for src, dst in zip(refs[: len(refs) // 2], refs[len(refs) // 2 :]):
        dst[...] = src[...]


def hold(*arrays):
    return pl.pallas_call(
        hold_kernel,
        out_shape=[jax.ShapeDtypeStruct(a.shape, a.dtype) for a in arrays],
        in_specs=[inside()] * len(arrays),
        out_specs=[inside()] * len(arrays),
        compiler_params=pltpu.CompilerParams(vmem_limit_bytes=4 << 20),
        name="hold",
    )(*arrays)


def join_kernel(axis, *refs):
    out, start = refs[-1], 0
    for piece in refs[:-1]:
        if axis == 0:
            n = out.shape[0] // (len(refs) - 1)
            out[start : start + n, :] = piece[0:n, :]
        else:
            n = piece.shape[1]
            out[:, start : start + n] = piece[...]
        start += n


def join(axis, pieces, n):
    shape = list(pieces[0].shape)
    shape[axis] = n * len(pieces)
    return pl.pallas_call(
        functools.partial(join_kernel, axis),
        out_shape=jax.ShapeDtypeStruct(tuple(shape), jnp.bfloat16),
        in_specs=[inside()] * len(pieces),
        out_specs=inside(),
        compiler_params=pltpu.CompilerParams(vmem_limit_bytes=4 << 20),
    )(*pieces)


def gather_kernel(places, tokens, slots, refs, keys, values, usable):
    block = len(places) * tokens
    n = keys.shape[1]
    for i, (which, row, col) in enumerate(places):
        kv, cols = refs[which], slice(col, col + n)
        at = slice(i * tokens, (i + 1) * tokens)
        keys[at, :] = kv[row : row + tokens, cols]
        values[at, :] = kv[row + tokens : row + 2 * tokens, cols]
        at = slice(block + i * slots, block + (i + 1) * slots)
        row += 2 * tokens
        keys[at, :] = kv[row : row + slots, cols]
        values[at, :] = kv[row + slots : row + 2 * slots, cols]
    lane = lax.broadcasted_iota(jnp.int32, (16, 128), 1)
    each = 128 // slots
    for start in range(0, len(places), each):
        flags = jnp.zeros((16, 128), jnp.float32)
        for j in range(each):
            which, row, _ = places[start + j]
            row += 2 * tokens + 2 * slots
            flag = refs[which][row : row + 16, 0:128].astype(jnp.float32)
            flags = jnp.where(lax.div(lane, slots) == j, flag, flags)
        usable[:, start * slots : start * slots + 128] = flags


def attend_rows(keys, values, usable, query, block, cols):
    scale = math.log2(math.e) / math.sqrt(DH)
    contract = (((1,), (1,)), ((), ()))
    main = lax.dot_general(
        query, keys[0:block, cols], contract, preferred_element_type=jnp.float32
    )
    tail = lax.dot_general(
        query, keys[block:, cols], contract, preferred_element_type=jnp.float32
    )
    tail = jnp.where(usable, tail, -3e38)
    top = jnp.maximum(jnp.max(main, axis=1, keepdims=True), jnp.max(tail, axis=1, keepdims=True))
    main = jnp.exp2((main - top) * scale)
    tail = jnp.exp2((tail - top) * scale)
    total = jnp.sum(main, axis=1, keepdims=True) + jnp.sum(tail, axis=1, keepdims=True)
    mixed = jnp.dot(
        main.astype(jnp.bfloat16), values[0:block, cols], preferred_element_type=jnp.float32
    ) + jnp.dot(tail.astype(jnp.bfloat16), values[block:, cols], preferred_element_type=jnp.float32)
    return (mixed / total).astype(jnp.bfloat16)


def attend_kernel(block, tokens, places, refs, keys, values, usable, outs, query):
    flags = usable[0:1, :] > 0.5
    n = keys.shape[1]
    for j, (which, row, col) in enumerate(places):
        query[j * tokens : (j + 1) * tokens, :] = refs[which][row : row + tokens, col : col + n]
    for h in range(n // DH):
        cols = slice(h * DH, (h + 1) * DH)
        step = min(2, len(places)) * tokens
        for start in range(0, len(places) * tokens, step):
            out = attend_rows(keys, values, flags, query[start : start + step, cols], block, cols)
            for row in range(0, step, tokens):
                outs[(start + row) // tokens][:, cols] = out[row : row + tokens]


def gather_and_attend_kernel(n_in, kv_places, q_places, tokens, slots, *refs):
    ins, outs = refs[:n_in], refs[n_in : n_in + len(q_places)]
    whole, query = refs[n_in + len(q_places) : -1], refs[-1]
    gather_kernel(kv_places, tokens, slots, ins, *whole)
    attend_kernel(len(kv_places) * tokens, tokens, q_places, ins, *whole, outs, query)


def gather_and_attend(arrays, kv_places, q_places, width, tokens, slots):
    rows = len(kv_places) * (tokens + slots)
    out = jax.ShapeDtypeStruct((tokens, width), jnp.bfloat16)
    rows_kept = jax.ShapeDtypeStruct((rows, width), jnp.bfloat16)
    flags = jax.ShapeDtypeStruct((16, len(kv_places) * slots), jnp.float32)
    made = pl.pallas_call(
        functools.partial(
            gather_and_attend_kernel, len(arrays), tuple(kv_places), tuple(q_places), tokens, slots
        ),
        out_shape=[out] * len(q_places) + [rows_kept, rows_kept, flags],
        in_specs=[inside()] * len(arrays),
        out_specs=[inside()] * (len(q_places) + 3),
        scratch_shapes=[pltpu.VMEM((len(q_places) * tokens, width), jnp.bfloat16)],
        compiler_params=pltpu.CompilerParams(vmem_limit_bytes=20 << 20),
        name="gather_and_attend",
    )(*arrays)
    return made[: len(q_places)], made[len(q_places) :]


def kept_attend_kernel(block, tokens, places, *refs):
    n = len(places)
    attend_kernel(block, tokens, places, refs[3:-1 - n], *refs[:3], refs[-1 - n : -1], refs[-1])


def attend(kept, qs, places, tokens):
    width, rows = kept[0].shape[1], kept[0].shape[0]
    block = rows - kept[2].shape[1]
    return pl.pallas_call(
        functools.partial(kept_attend_kernel, block, tokens, tuple(places)),
        out_shape=[jax.ShapeDtypeStruct((tokens, width), jnp.bfloat16)] * len(places),
        in_specs=[inside()] * (3 + len(qs)),
        out_specs=[inside()] * len(places),
        scratch_shapes=[pltpu.VMEM((len(places) * tokens, width), jnp.bfloat16)],
        compiler_params=pltpu.CompilerParams(vmem_limit_bytes=16 << 20),
        name="attend",
    )(*kept, *qs)


def stage_kernel(seq, width, start, each, count, by_core, other, w, out, sems):
    me = lax.div(lax.axis_index("seq"), seq // GROUPS)
    x = lax.axis_index("head")
    half = lax.bitwise_xor(x, 1) if other else x
    n = out.shape[1]
    cols = pl.ds(pl.multiple_of(half * n, n), n)
    base = count * lax.rem(lax.axis_index("seq"), CORES) if by_core else 0
    copies = []
    for j in range(count):
        group = lax.bitwise_xor(me, base + j)
        rows = pl.ds(pl.multiple_of(group * width + start, 128), each)
        copies.append(
            pltpu.make_async_copy(w.at[rows, cols], out.at[pl.ds(j * each, each), :], sems.at[j])
        )
    for copy in copies:
        copy.start()
    for copy in copies:
        copy.wait()


def stage(seq, width, start, each, count, by_core, other, w):
    return pl.pallas_call(
        functools.partial(stage_kernel, seq, width, start, each, count, by_core, other),
        out_shape=jax.ShapeDtypeStruct((count * each, w.shape[1] // 2), w.dtype),
        in_specs=[outside()],
        out_specs=inside(),
        scratch_shapes=[pltpu.SemaphoreType.DMA((count,))],
        compiler_params=pltpu.CompilerParams(vmem_limit_bytes=45 << 20),
    )(w)


def project_kernel(start, n_parts, *refs):
    parts, w, out = refs[:n_parts], refs[n_parts], refs[n_parts + 1]
    n = out.shape[1]
    attended = jnp.concatenate([p[...] for p in parts], axis=1)
    out[...] = jnp.dot(
        attended, w[:, start : start + n], preferred_element_type=jnp.float32
    ).astype(out.dtype)


def project(parts, w, start, n, dtype):
    return pl.pallas_call(
        functools.partial(project_kernel, start, len(parts)),
        out_shape=jax.ShapeDtypeStruct((parts[0].shape[0], n), dtype),
        in_specs=[inside()] * (len(parts) + 1),
        out_specs=inside(),
        compiler_params=pltpu.CompilerParams(vmem_limit_bytes=8 << 20),
        name="project",
    )(*parts, w)


def finish_kernel(own, attended, w_mine, w_near, *refs):
    out, start = refs[-1], 0
    n = w_mine.shape[0]
    core = lax.rem(lax.axis_index("seq"), CORES)
    mine = attended[:, pl.ds(pl.multiple_of(core * n, n), n)]
    near = attended[:, pl.ds(pl.multiple_of((1 - core) * n, n), n)]
    for piece in refs[:-1]:
        at = slice(start, start + piece.shape[1])
        total = own[:, at] + piece[...].astype(jnp.float32)
        total += jnp.dot(mine, w_mine[:, at], preferred_element_type=jnp.float32)
        total += jnp.dot(near, w_near[:, at], preferred_element_type=jnp.float32)
        out[:, at] = total.astype(out.dtype)
        start += piece.shape[1]


def finish(own, attended, w_mine, w_near, pieces):
    return pl.pallas_call(
        finish_kernel,
        out_shape=jax.ShapeDtypeStruct(own.shape, jnp.bfloat16),
        in_specs=[inside()] * (4 + len(pieces)),
        out_specs=inside(),
        compiler_params=pltpu.CompilerParams(vmem_limit_bytes=8 << 20),
        name="finish",
    )(own, attended, w_mine, w_near, *pieces)


def dealt_plan(
    seq, queries, block_keys, block_values, cache_keys, cache_values, cache_lengths, out_weight
):
    tokens, slots = queries.shape[0], cache_keys.shape[0]
    width = queries.shape[1] // GROUPS
    late = DH
    early = width - late
    stride = seq // GROUPS

    def over(x, flip):
        return lax.ppermute(x, "seq", [(s, s ^ flip) for s in range(seq)])

    def over_z(x, step):
        return over(x, step * stride)

    def over_x(x):
        return lax.ppermute(x, "head", [(0, 1), (1, 0)])

    (own_kv, own_q), first, last = pack(
        seq, width, late, cache_lengths, queries, block_keys, block_values, cache_keys, cache_values
    )
    steps = range(1, GROUPS)
    kvs = [over_z(first[2 * j - 2], j) for j in steps]
    qs = [over_z(first[2 * j - 1], j) for j in steps]
    ends = [over_z(last[j - 1], j) for j in steps]
    shipped = stage(seq, width, early, late, GROUPS // CORES, True, True, out_weight)
    w_mine = over_x(shipped)
    w_near = over(w_mine, 1)
    held_kv, held_q = hold(own_kv, own_q)
    gathered = []
    for i, kv in enumerate([own_kv] + kvs):
        far = over(kv, CORES)
        near, across = over(kv, 1), over(far, 1)
        gathered += [held_kv if i == 0 else kv, near, far, across]
    owns = gathered[:4]
    n = len(gathered)
    far_parts, kept = gather_and_attend(
        gathered + qs[1:],
        [(i, 0, 0) for i in range(n)],
        [(n, 0, 0), (n + 1, 0, 0)],
        early,
        tokens,
        slots,
    )
    near_parts = attend(kept, [held_q, qs[0]], [(0, 0, 0), (1, 0, 0)], tokens)
    parts = [near_parts[0], over_z(near_parts[1], 1)]
    parts += [over_z(far_parts[j], j + 2) for j in range(2)]
    rows = 2 * tokens + 2 * slots + 16
    joined = join(0, ends, rows)
    far = over(joined, CORES)
    near, across = over(joined, 1), over(far, 1)
    places = [(i, 0, early) for i in range(4)]
    places += [(4 + i, j * rows, 0) for i in range(4) for j in range(GROUPS - 1)]
    end_parts, _ = gather_and_attend(
        owns + [joined, near, far, across, held_q] + ends,
        places,
        [(8, 0, early)] + [(9 + j, rows, 0) for j in range(GROUPS - 1)],
        late,
        tokens,
        slots,
    )
    end_parts = [end_parts[0]] + [over_z(end_parts[j], j) for j in steps]
    half = out_weight.shape[1] // 2
    w_other = stage(seq, width, 0, early, GROUPS, False, True, out_weight)
    cuts = [0, half // 4, half]
    arrived = []
    for i in range(len(cuts) - 1):
        theirs = project(parts, w_other, cuts[i], cuts[i + 1] - cuts[i], jnp.bfloat16)
        arrived.append(over_x(theirs))
    ending = join(1, end_parts, late)
    attended = over_x(ending)
    w_own = stage(seq, width, 0, width, GROUPS, False, False, out_weight)
    both = [p for pair in zip(parts, end_parts) for p in pair]
    own = project(both, w_own, 0, half, jnp.float32)
    return finish(own, attended, w_mine, w_near, arrived)


def on_device(seq, head, *args):
    queries, cache_keys = args[0], args[3]
    heads_here = queries.shape[1] // DH
    slots = cache_keys.shape[0]
    rows_y = seq // (GROUPS * CORES)
    fits = (
        head == 2
        and seq % (GROUPS * CORES) == 0
        and rows_y == 2
        and heads_here % GROUPS == 0
        and heads_here > GROUPS
        and slots == 16
        and (seq * slots) % 128 == 0
        and queries.shape[0] % 16 == 0
        and args[6].shape[1] % 1024 == 0
    )
    return dealt_plan(seq, *args) if fits else gathered_plan(*args)


def solution(mesh):
    return jax.shard_map(
        functools.partial(on_device, mesh.shape["seq"], mesh.shape["head"]),
        mesh=mesh,
        in_specs=(
            P("seq", "head"),
            P("seq", "head"),
            P("seq", "head"),
            P("seq", "head"),
            P("seq", "head"),
            P("seq"),
            P("head", None),
        ),
        out_specs=P("seq", "head"),
        check_vma=False,
    )
```

```python
import functools
import math

import jax
import jax.numpy as jnp
from jax import lax
from jax.experimental import pallas as pl
from jax.experimental.pallas import tpu as pltpu
from jax.sharding import PartitionSpec as P

DH = 128
NEG_BIG = -1e30
CORES = 2
SOON = 2
GROUPS = 4


def fold_keys(running, query_heads, key_rows, value_rows, usable):
    maxima, totals, accumulated = running
    heads_here = query_heads.shape[1]
    head_width = query_heads.shape[2]
    key_heads = key_rows.reshape(key_rows.shape[0], heads_here, head_width)
    value_heads = value_rows.reshape(value_rows.shape[0], heads_here, head_width)
    scores = jnp.einsum(
        "qhd,khd->hqk", query_heads, key_heads, preferred_element_type=jnp.float32
    ) * (1.0 / math.sqrt(head_width))
    if usable is not None:
        scores = jnp.where(usable[None, None, :], scores, NEG_BIG)
    newest = jnp.maximum(maxima, jnp.max(scores, axis=2))
    carried = jnp.exp(maxima - newest)
    weights = jnp.exp(scores - newest[:, :, None])
    totals = totals * carried + jnp.sum(weights, axis=2)
    mixed = jnp.einsum(
        "hqk,khd->hqd",
        weights.astype(jnp.bfloat16),
        value_heads,
        preferred_element_type=jnp.float32,
    )
    accumulated = accumulated * carried[:, :, None] + mixed
    return (newest, totals, accumulated)


def cache_usable(lengths_piece, slots, row_count):
    slot_index = jnp.arange(row_count, dtype=jnp.int32) % slots
    slot_limit = jnp.repeat(lengths_piece.astype(jnp.int32), slots, total_repeat_length=row_count)
    return slot_index < slot_limit


def gathered_plan(
    queries, block_keys, block_values, cache_keys, cache_values, cache_lengths, out_weight
):
    tokens_here = queries.shape[0]
    heads_here = queries.shape[1] // DH
    query_heads = queries.reshape(tokens_here, heads_here, DH)
    slots = cache_keys.shape[0]
    running = (
        jnp.full((heads_here, tokens_here), NEG_BIG, jnp.float32),
        jnp.zeros((heads_here, tokens_here), jnp.float32),
        jnp.zeros((heads_here, tokens_here, DH), jnp.float32),
    )
    gather = functools.partial(lax.all_gather, axis_name="seq", axis=0, tiled=True)
    running = fold_keys(running, query_heads, gather(block_keys), gather(block_values), None)
    cached = gather(cache_keys)
    usable = cache_usable(gather(cache_lengths), slots, cached.shape[0])
    running = fold_keys(running, query_heads, cached, gather(cache_values), usable)
    _, totals, accumulated = running
    attended = (
        (accumulated / totals[:, :, None])
        .transpose(1, 0, 2)
        .reshape(tokens_here, heads_here * DH)
        .astype(jnp.bfloat16)
    )
    partial_terms = jnp.dot(attended, out_weight, preferred_element_type=jnp.float32)
    return lax.psum_scatter(
        partial_terms.astype(jnp.bfloat16), "head", scatter_dimension=1, tiled=True
    )


def inside():
    return pl.BlockSpec(memory_space=pltpu.VMEM)


def outside():
    return pl.BlockSpec(memory_space=pltpu.HBM)


def pack_kernel(seq, width, late, slots, len_ref, q, k, v, ck, cv, *refs):
    outs, sems = refs[:-1], refs[-1]
    own_kv, own_q = outs[:2]
    first, last = outs[2 : 2 * GROUPS], outs[2 * GROUPS :]
    me = lax.div(lax.axis_index("seq"), seq // GROUPS)
    copies = []

    def cut(kv, group, start, n):
        cols = pl.ds(pl.multiple_of(group * width + start, 128), n)
        row = 0
        for src in (k, v, ck, cv):
            rows = src.shape[0]
            copies.append((src.at[:, cols], kv.at[pl.ds(row, rows), :]))
            row += rows
        return cols

    for step in range(1, GROUPS):
        kv, qo = first[2 * step - 2], first[2 * step - 1]
        cols = cut(kv, lax.bitwise_xor(me, step), 0, width - late)
        copies.append((q.at[:, cols], qo))
    copies.append((q.at[:, cut(own_kv, me, 0, width)], own_q))
    for step in range(1, GROUPS):
        kv = last[step - 1]
        cols = cut(kv, lax.bitwise_xor(me, step), width - late, late)
        tokens = q.shape[0]
        copies.append((q.at[:, cols], kv.at[pl.ds(kv.shape[0] - tokens, tokens), :]))
    started = [
        pltpu.make_async_copy(src, dst, sems.at[i]) for i, (src, dst) in enumerate(copies)
    ]
    for copy in started:
        copy.start()
    row = 2 * k.shape[0] + 2 * slots
    for kv in (own_kv, *first[::2], *last):
        lane = lax.broadcasted_iota(jnp.int32, (16, kv.shape[1]), 1)
        kv[row : row + 16, :] = jnp.where(lax.rem(lane, slots) < len_ref[0], 1.0, 0.0).astype(
            jnp.bfloat16
        )
    for copy in started:
        copy.wait()


def pack(seq, width, late, lengths, q, k, v, ck, cv):
    tokens, slots = q.shape[0], ck.shape[0]
    rows = 2 * tokens + 2 * slots + 16

    def array(n, columns):
        return jax.ShapeDtypeStruct((n, columns), jnp.bfloat16)

    shapes = [array(rows, width), array(tokens, width)]
    shapes += [array(rows, width - late), array(tokens, width - late)] * (GROUPS - 1)
    shapes += [array(rows + tokens, late)] * (GROUPS - 1)
    made = pl.pallas_call(
        functools.partial(pack_kernel, seq, width, late, slots),
        out_shape=shapes,
        in_specs=[pl.BlockSpec(memory_space=pltpu.SMEM)] + [outside()] * 5,
        out_specs=[inside()] * len(shapes),
        scratch_shapes=[pltpu.SemaphoreType.DMA((5 * (2 * GROUPS - 1),))],
        compiler_params=pltpu.CompilerParams(vmem_limit_bytes=61 << 20),
        name="pack",
    )(lengths, q, k, v, ck, cv)
    return made[:2], made[2 : 2 * GROUPS], made[2 * GROUPS :]


def hold_kernel(*refs):
    for src, dst in zip(refs[: len(refs) // 2], refs[len(refs) // 2 :]):
        dst[...] = src[...]


def hold(*arrays):
    return pl.pallas_call(
        hold_kernel,
        out_shape=[jax.ShapeDtypeStruct(a.shape, a.dtype) for a in arrays],
        in_specs=[inside()] * len(arrays),
        out_specs=[inside()] * len(arrays),
        compiler_params=pltpu.CompilerParams(vmem_limit_bytes=4 << 20),
        name="hold",
    )(*arrays)


def join_kernel(axis, *refs):
    out, start = refs[-1], 0
    for piece in refs[:-1]:
        if axis == 0:
            n = out.shape[0] // (len(refs) - 1)
            out[start : start + n, :] = piece[0:n, :]
        else:
            n = piece.shape[1]
            out[:, start : start + n] = piece[...]
        start += n


def join(axis, pieces, n):
    shape = list(pieces[0].shape)
    shape[axis] = n * len(pieces)
    return pl.pallas_call(
        functools.partial(join_kernel, axis),
        out_shape=jax.ShapeDtypeStruct(tuple(shape), jnp.bfloat16),
        in_specs=[inside()] * len(pieces),
        out_specs=inside(),
        compiler_params=pltpu.CompilerParams(vmem_limit_bytes=4 << 20),
    )(*pieces)


def gather_kernel(places, tokens, slots, refs, keys, values, usable):
    block = len(places) * tokens
    n = keys.shape[1]
    for i, (which, row, col) in enumerate(places):
        kv, cols = refs[which], slice(col, col + n)
        at = slice(i * tokens, (i + 1) * tokens)
        keys[at, :] = kv[row : row + tokens, cols]
        values[at, :] = kv[row + tokens : row + 2 * tokens, cols]
        at = slice(block + i * slots, block + (i + 1) * slots)
        row += 2 * tokens
        keys[at, :] = kv[row : row + slots, cols]
        values[at, :] = kv[row + slots : row + 2 * slots, cols]
    lane = lax.broadcasted_iota(jnp.int32, (16, 128), 1)
    each = 128 // slots
    for start in range(0, len(places), each):
        flags = jnp.zeros((16, 128), jnp.float32)
        for j in range(each):
            which, row, _ = places[start + j]
            row += 2 * tokens + 2 * slots
            flag = refs[which][row : row + 16, 0:128].astype(jnp.float32)
            flags = jnp.where(lax.div(lane, slots) == j, flag, flags)
        usable[:, start * slots : start * slots + 128] = flags


def attend_rows(keys, values, usable, query, block, cols):
    scale = math.log2(math.e) / math.sqrt(DH)
    contract = (((1,), (1,)), ((), ()))
    main = lax.dot_general(
        query, keys[0:block, cols], contract, preferred_element_type=jnp.float32
    )
    tail = lax.dot_general(
        query, keys[block:, cols], contract, preferred_element_type=jnp.float32
    )
    tail = jnp.where(usable, tail, -3e38)
    top = jnp.maximum(jnp.max(main, axis=1, keepdims=True), jnp.max(tail, axis=1, keepdims=True))
    main = jnp.exp2((main - top) * scale)
    tail = jnp.exp2((tail - top) * scale)
    total = jnp.sum(main, axis=1, keepdims=True) + jnp.sum(tail, axis=1, keepdims=True)
    mixed = jnp.dot(
        main.astype(jnp.bfloat16), values[0:block, cols], preferred_element_type=jnp.float32
    ) + jnp.dot(tail.astype(jnp.bfloat16), values[block:, cols], preferred_element_type=jnp.float32)
    return (mixed / total).astype(jnp.bfloat16)


def attend_kernel(block, tokens, places, refs, keys, values, usable, outs, query):
    flags = usable[0:1, :] > 0.5
    n = keys.shape[1]
    for j, (which, row, col) in enumerate(places):
        query[j * tokens : (j + 1) * tokens, :] = refs[which][row : row + tokens, col : col + n]
    for h in range(n // DH):
        cols = slice(h * DH, (h + 1) * DH)
        step = min(2, len(places)) * tokens
        for start in range(0, len(places) * tokens, step):
            out = attend_rows(keys, values, flags, query[start : start + step, cols], block, cols)
            for row in range(0, step, tokens):
                outs[(start + row) // tokens][:, cols] = out[row : row + tokens]


def gather_and_attend_kernel(n_in, kv_places, q_places, tokens, slots, *refs):
    ins, outs = refs[:n_in], refs[n_in : n_in + len(q_places)]
    whole, query = refs[n_in + len(q_places) : -1], refs[-1]
    gather_kernel(kv_places, tokens, slots, ins, *whole)
    attend_kernel(len(kv_places) * tokens, tokens, q_places, ins, *whole, outs, query)


def gather_and_attend(arrays, kv_places, q_places, width, tokens, slots):
    rows = len(kv_places) * (tokens + slots)
    out = jax.ShapeDtypeStruct((tokens, width), jnp.bfloat16)
    rows_kept = jax.ShapeDtypeStruct((rows, width), jnp.bfloat16)
    flags = jax.ShapeDtypeStruct((16, len(kv_places) * slots), jnp.float32)
    made = pl.pallas_call(
        functools.partial(
            gather_and_attend_kernel, len(arrays), tuple(kv_places), tuple(q_places), tokens, slots
        ),
        out_shape=[out] * len(q_places) + [rows_kept, rows_kept, flags],
        in_specs=[inside()] * len(arrays),
        out_specs=[inside()] * (len(q_places) + 3),
        scratch_shapes=[pltpu.VMEM((len(q_places) * tokens, width), jnp.bfloat16)],
        compiler_params=pltpu.CompilerParams(vmem_limit_bytes=20 << 20),
        name="gather_and_attend",
    )(*arrays)
    return made[: len(q_places)], made[len(q_places) :]


def kept_attend_kernel(block, tokens, places, *refs):
    n = len(places)
    attend_kernel(block, tokens, places, refs[3:-1 - n], *refs[:3], refs[-1 - n : -1], refs[-1])


def attend(kept, qs, places, tokens):
    width, rows = kept[0].shape[1], kept[0].shape[0]
    block = rows - kept[2].shape[1]
    return pl.pallas_call(
        functools.partial(kept_attend_kernel, block, tokens, tuple(places)),
        out_shape=[jax.ShapeDtypeStruct((tokens, width), jnp.bfloat16)] * len(places),
        in_specs=[inside()] * (3 + len(qs)),
        out_specs=[inside()] * len(places),
        scratch_shapes=[pltpu.VMEM((len(places) * tokens, width), jnp.bfloat16)],
        compiler_params=pltpu.CompilerParams(vmem_limit_bytes=16 << 20),
        name="attend",
    )(*kept, *qs)


def stage_kernel(seq, width, start, each, count, by_core, other, w, out, sems):
    me = lax.div(lax.axis_index("seq"), seq // GROUPS)
    x = lax.axis_index("head")
    half = lax.bitwise_xor(x, 1) if other else x
    n = out.shape[1]
    cols = pl.ds(pl.multiple_of(half * n, n), n)
    base = count * lax.rem(lax.axis_index("seq"), CORES) if by_core else 0
    copies = []
    for j in range(count):
        group = lax.bitwise_xor(me, base + j)
        rows = pl.ds(pl.multiple_of(group * width + start, 128), each)
        copies.append(
            pltpu.make_async_copy(w.at[rows, cols], out.at[pl.ds(j * each, each), :], sems.at[j])
        )
    for copy in copies:
        copy.start()
    for copy in copies:
        copy.wait()


def stage(seq, width, start, each, count, by_core, other, w):
    return pl.pallas_call(
        functools.partial(stage_kernel, seq, width, start, each, count, by_core, other),
        out_shape=jax.ShapeDtypeStruct((count * each, w.shape[1] // 2), w.dtype),
        in_specs=[outside()],
        out_specs=inside(),
        scratch_shapes=[pltpu.SemaphoreType.DMA((count,))],
        compiler_params=pltpu.CompilerParams(vmem_limit_bytes=45 << 20),
    )(w)


def project_kernel(seq, width, other, start, n_parts, *refs):
    parts, w, out = refs[:n_parts], refs[n_parts], refs[n_parts + 1]
    me = lax.div(lax.axis_index("seq"), seq // GROUPS)
    x = lax.axis_index("head")
    half = lax.bitwise_xor(x, 1) if other else x
    n = out.shape[1]
    cols = pl.ds(pl.multiple_of(half * (w.shape[1] // 2) + start, 128), n)
    total = None
    for j in range(GROUPS):
        group = parts[j * n_parts // GROUPS : (j + 1) * n_parts // GROUPS]
        attended = group[0][...]
        if len(group) > 1:
            attended = jnp.concatenate([p[...] for p in group], axis=1)
        first = pl.multiple_of(lax.bitwise_xor(me, j) * width, 128)
        rows = w[pl.ds(first, attended.shape[1]), cols]
        term = jnp.dot(attended, rows, preferred_element_type=jnp.float32)
        total = term if total is None else total + term
    out[...] = total.astype(out.dtype)


def project(seq, width, other, parts, w, start, n, dtype):
    return pl.pallas_call(
        functools.partial(project_kernel, seq, width, other, start, len(parts)),
        out_shape=jax.ShapeDtypeStruct((parts[0].shape[0], n), dtype),
        in_specs=[inside()] * (len(parts) + 1),
        out_specs=inside(),
        compiler_params=pltpu.CompilerParams(vmem_limit_bytes=8 << 20),
        name="project",
    )(*parts, w)


def finish_kernel(n_pieces, order, own, w_mine, w_near, *refs):
    pieces, theirs, out, attended = refs[:n_pieces], refs[n_pieces:-2], refs[-2], refs[-1]
    n = w_mine.shape[0]
    each = n * CORES // len(order)
    for i, place in enumerate(order):
        per = len(order) // n_pieces
        at = slice(i % per * each, (i % per + 1) * each)
        attended[:, place * each : (place + 1) * each] = pieces[i // per][:, at]
    core = lax.rem(lax.axis_index("seq"), CORES)
    mine = attended[:, pl.ds(pl.multiple_of(core * n, n), n)]
    near = attended[:, pl.ds(pl.multiple_of((1 - core) * n, n), n)]
    start = 0
    for piece in theirs:
        at = slice(start, start + piece.shape[1])
        total = own[:, at] + piece[...].astype(jnp.float32)
        total += jnp.dot(mine, w_mine[:, at], preferred_element_type=jnp.float32)
        total += jnp.dot(near, w_near[:, at], preferred_element_type=jnp.float32)
        out[:, at] = total.astype(out.dtype)
        start += piece.shape[1]


def finish(own, attended, order, w_mine, w_near, theirs):
    return pl.pallas_call(
        functools.partial(finish_kernel, len(attended), tuple(order)),
        out_shape=jax.ShapeDtypeStruct(own.shape, jnp.bfloat16),
        in_specs=[inside()] * (3 + len(attended) + len(theirs)),
        out_specs=inside(),
        scratch_shapes=[pltpu.VMEM((own.shape[0], w_mine.shape[0] * CORES), jnp.bfloat16)],
        compiler_params=pltpu.CompilerParams(vmem_limit_bytes=8 << 20),
        name="finish",
    )(own, w_mine, w_near, *attended, *theirs)


def dealt_plan(
    seq, queries, block_keys, block_values, cache_keys, cache_values, cache_lengths, out_weight
):
    tokens, slots = queries.shape[0], cache_keys.shape[0]
    width = queries.shape[1] // GROUPS
    late = DH
    early = width - late
    stride = seq // GROUPS

    def over(x, flip):
        return lax.ppermute(x, "seq", [(s, s ^ flip) for s in range(seq)])

    def over_z(x, step):
        return over(x, step * stride)

    def over_x(x):
        return lax.ppermute(x, "head", [(0, 1), (1, 0)])

    (own_kv, own_q), first, last = pack(
        seq, width, late, cache_lengths, queries, block_keys, block_values, cache_keys, cache_values
    )
    steps = range(1, GROUPS)
    kvs = [over_z(first[2 * j - 2], j) for j in steps]
    qs = [over_z(first[2 * j - 1], j) for j in steps]
    ends = [over_z(last[j - 1], j) for j in steps]
    shipped = stage(seq, width, early, late, GROUPS // CORES, True, True, out_weight)
    w_mine = over_x(shipped)
    w_near = over(w_mine, 1)
    held_kv, held_q = hold(own_kv, own_q)
    gathered = []
    for i, kv in enumerate([own_kv] + kvs):
        far = over(kv, CORES)
        near, across = over(kv, 1), over(far, 1)
        gathered += [held_kv if i == 0 else kv, near, far, across]
    owns = gathered[:4]
    n = len(gathered)
    far_parts, kept = gather_and_attend(
        gathered + qs[1:],
        [(i, 0, 0) for i in range(n)],
        [(n, 0, 0), (n + 1, 0, 0)],
        early,
        tokens,
        slots,
    )
    near_parts = attend(kept, [held_q, qs[0]], [(0, 0, 0), (1, 0, 0)], tokens)
    parts = [near_parts[0], over_z(near_parts[1], 1)]
    parts += [over_z(far_parts[j], j + 2) for j in range(2)]
    rows = 2 * tokens + 2 * slots + 16
    joined = join(0, ends[1:], rows)
    pieces = []
    for piece in (ends[0], joined):
        far = over(piece, CORES)
        near, across = over(piece, 1), over(far, 1)
        pieces += [piece, near, far, across]
    places = [(i, 0, early) for i in range(4)] + [(4 + i, 0, 0) for i in range(4)]
    places += [(8 + i, j * rows, 0) for i in range(4) for j in range(GROUPS - 2)]
    end_parts, _ = gather_and_attend(
        owns + pieces + [held_q] + ends[1:],
        places,
        [(12, 0, early), (4, rows, 0)] + [(13 + j, rows, 0) for j in range(GROUPS - 2)],
        late,
        tokens,
        slots,
    )
    end_parts = [end_parts[0]] + [over_z(end_parts[j], j) for j in steps]
    half = out_weight.shape[1] // 2
    cuts = [0, half // 4, half]
    arrived = []
    for i in range(len(cuts) - 1):
        theirs = project(
            seq, width, True, parts, out_weight, cuts[i], cuts[i + 1] - cuts[i], jnp.bfloat16
        )
        arrived.append(over_x(theirs))
    order = (0, SOON, *(j for j in steps if j != SOON))
    attended = []
    for i in range(2):
        ending = join(1, [end_parts[j] for j in order[2 * i : 2 * i + 2]], late)
        attended.append(over_x(ending))
    both = [p for pair in zip(parts, end_parts) for p in pair]
    own = project(seq, width, False, both, out_weight, 0, half, jnp.float32)
    return finish(own, attended, order, w_mine, w_near, arrived)


def on_device(seq, head, *args):
    queries, cache_keys = args[0], args[3]
    heads_here = queries.shape[1] // DH
    slots = cache_keys.shape[0]
    rows_y = seq // (GROUPS * CORES)
    fits = (
        head == 2
        and seq % (GROUPS * CORES) == 0
        and rows_y == 2
        and heads_here % GROUPS == 0
        and heads_here > GROUPS
        and slots == 16
        and (seq * slots) % 128 == 0
        and queries.shape[0] % 16 == 0
        and args[6].shape[1] % 1024 == 0
    )
    return dealt_plan(seq, *args) if fits else gathered_plan(*args)


def solution(mesh):
    return jax.shard_map(
        functools.partial(on_device, mesh.shape["seq"], mesh.shape["head"]),
        mesh=mesh,
        in_specs=(
            P("seq", "head"),
            P("seq", "head"),
            P("seq", "head"),
            P("seq", "head"),
            P("seq", "head"),
            P("seq"),
            P("head", None),
        ),
        out_specs=P("seq", "head"),
        check_vma=False,
    )
```

```python
import functools
import math

import jax
import jax.numpy as jnp
from jax import lax
from jax.experimental import pallas as pl
from jax.experimental.pallas import tpu as pltpu
from jax.sharding import PartitionSpec as P

DH = 128
NEG_BIG = -1e30
CORES = 2
SOON = 2
GROUPS = 4


def fold_keys(running, query_heads, key_rows, value_rows, usable):
    maxima, totals, accumulated = running
    heads_here = query_heads.shape[1]
    head_width = query_heads.shape[2]
    key_heads = key_rows.reshape(key_rows.shape[0], heads_here, head_width)
    value_heads = value_rows.reshape(value_rows.shape[0], heads_here, head_width)
    scores = jnp.einsum(
        "qhd,khd->hqk", query_heads, key_heads, preferred_element_type=jnp.float32
    ) * (1.0 / math.sqrt(head_width))
    if usable is not None:
        scores = jnp.where(usable[None, None, :], scores, NEG_BIG)
    newest = jnp.maximum(maxima, jnp.max(scores, axis=2))
    carried = jnp.exp(maxima - newest)
    weights = jnp.exp(scores - newest[:, :, None])
    totals = totals * carried + jnp.sum(weights, axis=2)
    mixed = jnp.einsum(
        "hqk,khd->hqd",
        weights.astype(jnp.bfloat16),
        value_heads,
        preferred_element_type=jnp.float32,
    )
    accumulated = accumulated * carried[:, :, None] + mixed
    return (newest, totals, accumulated)


def cache_usable(lengths_piece, slots, row_count):
    slot_index = jnp.arange(row_count, dtype=jnp.int32) % slots
    slot_limit = jnp.repeat(lengths_piece.astype(jnp.int32), slots, total_repeat_length=row_count)
    return slot_index < slot_limit


def gathered_plan(
    queries, block_keys, block_values, cache_keys, cache_values, cache_lengths, out_weight
):
    tokens_here = queries.shape[0]
    heads_here = queries.shape[1] // DH
    query_heads = queries.reshape(tokens_here, heads_here, DH)
    slots = cache_keys.shape[0]
    running = (
        jnp.full((heads_here, tokens_here), NEG_BIG, jnp.float32),
        jnp.zeros((heads_here, tokens_here), jnp.float32),
        jnp.zeros((heads_here, tokens_here, DH), jnp.float32),
    )
    gather = functools.partial(lax.all_gather, axis_name="seq", axis=0, tiled=True)
    running = fold_keys(running, query_heads, gather(block_keys), gather(block_values), None)
    cached = gather(cache_keys)
    usable = cache_usable(gather(cache_lengths), slots, cached.shape[0])
    running = fold_keys(running, query_heads, cached, gather(cache_values), usable)
    _, totals, accumulated = running
    attended = (
        (accumulated / totals[:, :, None])
        .transpose(1, 0, 2)
        .reshape(tokens_here, heads_here * DH)
        .astype(jnp.bfloat16)
    )
    partial_terms = jnp.dot(attended, out_weight, preferred_element_type=jnp.float32)
    return lax.psum_scatter(
        partial_terms.astype(jnp.bfloat16), "head", scatter_dimension=1, tiled=True
    )


def inside():
    return pl.BlockSpec(memory_space=pltpu.VMEM)


def outside():
    return pl.BlockSpec(memory_space=pltpu.HBM)


def pack_kernel(seq, width, late, slots, len_ref, q, k, v, ck, cv, *refs):
    outs, sems = refs[:-1], refs[-1]
    own_kv, own_q = outs[:2]
    first, last = outs[2 : 2 * GROUPS], outs[2 * GROUPS :]
    me = lax.div(lax.axis_index("seq"), seq // GROUPS)
    copies = []

    def cut(kv, group, start, n):
        cols = pl.ds(pl.multiple_of(group * width + start, 128), n)
        row = 0
        for src in (k, v, ck, cv):
            rows = src.shape[0]
            copies.append((src.at[:, cols], kv.at[pl.ds(row, rows), :]))
            row += rows
        return cols

    for step in range(1, GROUPS):
        kv, qo = first[2 * step - 2], first[2 * step - 1]
        cols = cut(kv, lax.bitwise_xor(me, step), 0, width - late)
        copies.append((q.at[:, cols], qo))
    copies.append((q.at[:, cut(own_kv, me, 0, width)], own_q))
    for step in range(1, GROUPS):
        kv = last[step - 1]
        cols = cut(kv, lax.bitwise_xor(me, step), width - late, late)
        tokens = q.shape[0]
        copies.append((q.at[:, cols], kv.at[pl.ds(kv.shape[0] - tokens, tokens), :]))
    started = [
        pltpu.make_async_copy(src, dst, sems.at[i]) for i, (src, dst) in enumerate(copies)
    ]
    for copy in started:
        copy.start()
    row = 2 * k.shape[0] + 2 * slots
    for kv in (own_kv, *first[::2]):
        lane = lax.broadcasted_iota(jnp.int32, (16, kv.shape[1]), 1)
        kv[row : row + 16, :] = jnp.where(lax.rem(lane, slots) < len_ref[0], 1.0, 0.0).astype(
            jnp.bfloat16
        )
    for copy in started:
        copy.wait()


def pack(seq, width, late, lengths, q, k, v, ck, cv):
    tokens, slots = q.shape[0], ck.shape[0]
    rows = 2 * tokens + 2 * slots + 16

    def array(n, columns):
        return jax.ShapeDtypeStruct((n, columns), jnp.bfloat16)

    shapes = [array(rows, width), array(tokens, width)]
    shapes += [array(rows, width - late), array(tokens, width - late)] * (GROUPS - 1)
    shapes += [array(rows - 16 + tokens, late)] * (GROUPS - 1)
    made = pl.pallas_call(
        functools.partial(pack_kernel, seq, width, late, slots),
        out_shape=shapes,
        in_specs=[pl.BlockSpec(memory_space=pltpu.SMEM)] + [outside()] * 5,
        out_specs=[inside()] * len(shapes),
        scratch_shapes=[pltpu.SemaphoreType.DMA((5 * (2 * GROUPS - 1),))],
        compiler_params=pltpu.CompilerParams(vmem_limit_bytes=61 << 20),
        name="pack",
    )(lengths, q, k, v, ck, cv)
    return made[:2], made[2 : 2 * GROUPS], made[2 * GROUPS :]


def hold_kernel(*refs):
    for src, dst in zip(refs[: len(refs) // 2], refs[len(refs) // 2 :]):
        dst[...] = src[...]


def hold(*arrays):
    return pl.pallas_call(
        hold_kernel,
        out_shape=[jax.ShapeDtypeStruct(a.shape, a.dtype) for a in arrays],
        in_specs=[inside()] * len(arrays),
        out_specs=[inside()] * len(arrays),
        compiler_params=pltpu.CompilerParams(vmem_limit_bytes=4 << 20),
        name="hold",
    )(*arrays)


def join_kernel(axis, *refs):
    out, start = refs[-1], 0
    for piece in refs[:-1]:
        if axis == 0:
            n = out.shape[0] // (len(refs) - 1)
            out[start : start + n, :] = piece[0:n, :]
        else:
            n = piece.shape[1]
            out[:, start : start + n] = piece[...]
        start += n


def join(axis, pieces, n):
    shape = list(pieces[0].shape)
    shape[axis] = n * len(pieces)
    return pl.pallas_call(
        functools.partial(join_kernel, axis),
        out_shape=jax.ShapeDtypeStruct(tuple(shape), jnp.bfloat16),
        in_specs=[inside()] * len(pieces),
        out_specs=inside(),
        compiler_params=pltpu.CompilerParams(vmem_limit_bytes=4 << 20),
    )(*pieces)


def gather_kernel(places, tokens, slots, refs, keys, values):
    block = len(places) * tokens
    n = keys.shape[1]
    for i, (which, row, col) in enumerate(places):
        kv, cols = refs[which], slice(col, col + n)
        at = slice(i * tokens, (i + 1) * tokens)
        keys[at, :] = kv[row : row + tokens, cols]
        values[at, :] = kv[row + tokens : row + 2 * tokens, cols]
        at = slice(block + i * slots, block + (i + 1) * slots)
        row += 2 * tokens
        keys[at, :] = kv[row : row + slots, cols]
        values[at, :] = kv[row + slots : row + 2 * slots, cols]


def flag_kernel(places, tokens, slots, refs, usable):
    lane = lax.broadcasted_iota(jnp.int32, (16, 128), 1)
    each = 128 // slots
    for start in range(0, len(places), each):
        flags = jnp.zeros((16, 128), jnp.float32)
        for j in range(each):
            which, row, _ = places[start + j]
            row += 2 * tokens + 2 * slots
            flag = refs[which][row : row + 16, 0:128].astype(jnp.float32)
            flags = jnp.where(lax.div(lane, slots) == j, flag, flags)
        usable[:, start * slots : start * slots + 128] = flags


def attend_rows(keys, values, usable, query, block, cols):
    scale = math.log2(math.e) / math.sqrt(DH)
    contract = (((1,), (1,)), ((), ()))
    main = lax.dot_general(
        query, keys[0:block, cols], contract, preferred_element_type=jnp.float32
    )
    tail = lax.dot_general(
        query, keys[block:, cols], contract, preferred_element_type=jnp.float32
    )
    tail = jnp.where(usable, tail, -3e38)
    top = jnp.maximum(jnp.max(main, axis=1, keepdims=True), jnp.max(tail, axis=1, keepdims=True))
    main = jnp.exp2((main - top) * scale)
    tail = jnp.exp2((tail - top) * scale)
    total = jnp.sum(main, axis=1, keepdims=True) + jnp.sum(tail, axis=1, keepdims=True)
    mixed = jnp.dot(
        main.astype(jnp.bfloat16), values[0:block, cols], preferred_element_type=jnp.float32
    ) + jnp.dot(tail.astype(jnp.bfloat16), values[block:, cols], preferred_element_type=jnp.float32)
    return (mixed / total).astype(jnp.bfloat16)


def attend_kernel(block, tokens, places, refs, keys, values, usable, outs, query):
    flags = usable[0:1, :] > 0.5
    n = keys.shape[1]
    for j, (which, row, col) in enumerate(places):
        query[j * tokens : (j + 1) * tokens, :] = refs[which][row : row + tokens, col : col + n]
    for h in range(n // DH):
        cols = slice(h * DH, (h + 1) * DH)
        step = min(2, len(places)) * tokens
        for start in range(0, len(places) * tokens, step):
            out = attend_rows(keys, values, flags, query[start : start + step, cols], block, cols)
            for row in range(0, step, tokens):
                outs[(start + row) // tokens][:, cols] = out[row : row + tokens]


def gather_and_attend_kernel(n_in, kv_places, q_places, tokens, slots, flagged, *refs):
    ins, outs = refs[:n_in], refs[n_in : n_in + len(q_places)]
    kept, query = refs[n_in + len(q_places) : -1], refs[-1]
    gather_kernel(kv_places, tokens, slots, ins, *kept[:2])
    if not flagged:
        flag_kernel(kv_places, tokens, slots, ins, kept[2])
    usable = ins[-1] if flagged else kept[2]
    attend_kernel(len(kv_places) * tokens, tokens, q_places, ins, *kept[:2], usable, outs, query)


def gather_and_attend(arrays, kv_places, q_places, width, tokens, slots, usable=None):
    flagged = usable is not None
    arrays = [*arrays, usable] if flagged else arrays
    rows = len(kv_places) * (tokens + slots)
    shapes = [jax.ShapeDtypeStruct((tokens, width), jnp.bfloat16)] * len(q_places)
    whole = [pltpu.VMEM((rows, width), jnp.bfloat16)] * 2
    if not flagged:
        shapes += [jax.ShapeDtypeStruct((rows, width), jnp.bfloat16)] * 2
        shapes += [jax.ShapeDtypeStruct((16, len(kv_places) * slots), jnp.float32)]
    made = pl.pallas_call(
        functools.partial(
            gather_and_attend_kernel,
            len(arrays),
            tuple(kv_places),
            tuple(q_places),
            tokens,
            slots,
            flagged,
        ),
        out_shape=shapes,
        in_specs=[inside()] * len(arrays),
        out_specs=[inside()] * len(shapes),
        scratch_shapes=whole * flagged
        + [pltpu.VMEM((len(q_places) * tokens, width), jnp.bfloat16)],
        compiler_params=pltpu.CompilerParams(vmem_limit_bytes=20 << 20),
        name="gather_and_attend",
    )(*arrays)
    return made[: len(q_places)], made[len(q_places) :]


def kept_attend_kernel(block, tokens, places, *refs):
    n = len(places)
    attend_kernel(block, tokens, places, refs[3:-1 - n], *refs[:3], refs[-1 - n : -1], refs[-1])


def attend(kept, qs, places, tokens):
    width, rows = kept[0].shape[1], kept[0].shape[0]
    block = rows - kept[2].shape[1]
    return pl.pallas_call(
        functools.partial(kept_attend_kernel, block, tokens, tuple(places)),
        out_shape=[jax.ShapeDtypeStruct((tokens, width), jnp.bfloat16)] * len(places),
        in_specs=[inside()] * (3 + len(qs)),
        out_specs=[inside()] * len(places),
        scratch_shapes=[pltpu.VMEM((len(places) * tokens, width), jnp.bfloat16)],
        compiler_params=pltpu.CompilerParams(vmem_limit_bytes=16 << 20),
        name="attend",
    )(*kept, *qs)


def stage_kernel(seq, width, start, each, count, by_core, other, w, out, sems):
    me = lax.div(lax.axis_index("seq"), seq // GROUPS)
    x = lax.axis_index("head")
    half = lax.bitwise_xor(x, 1) if other else x
    n = out.shape[1]
    cols = pl.ds(pl.multiple_of(half * n, n), n)
    base = count * lax.rem(lax.axis_index("seq"), CORES) if by_core else 0
    copies = []
    for j in range(count):
        group = lax.bitwise_xor(me, base + j)
        rows = pl.ds(pl.multiple_of(group * width + start, 128), each)
        copies.append(
            pltpu.make_async_copy(w.at[rows, cols], out.at[pl.ds(j * each, each), :], sems.at[j])
        )
    for copy in copies:
        copy.start()
    for copy in copies:
        copy.wait()


def stage(seq, width, start, each, count, by_core, other, w):
    return pl.pallas_call(
        functools.partial(stage_kernel, seq, width, start, each, count, by_core, other),
        out_shape=jax.ShapeDtypeStruct((count * each, w.shape[1] // 2), w.dtype),
        in_specs=[outside()],
        out_specs=inside(),
        scratch_shapes=[pltpu.SemaphoreType.DMA((count,))],
        compiler_params=pltpu.CompilerParams(vmem_limit_bytes=45 << 20),
    )(w)


def project_kernel(seq, width, other, start, n_parts, *refs):
    parts, w, out = refs[:n_parts], refs[n_parts], refs[n_parts + 1]
    me = lax.div(lax.axis_index("seq"), seq // GROUPS)
    x = lax.axis_index("head")
    half = lax.bitwise_xor(x, 1) if other else x
    n = out.shape[1]
    cols = pl.ds(pl.multiple_of(half * (w.shape[1] // 2) + start, 128), n)
    total = None
    for j in range(GROUPS):
        group = parts[j * n_parts // GROUPS : (j + 1) * n_parts // GROUPS]
        attended = group[0][...]
        if len(group) > 1:
            attended = jnp.concatenate([p[...] for p in group], axis=1)
        first = pl.multiple_of(lax.bitwise_xor(me, j) * width, 128)
        rows = w[pl.ds(first, attended.shape[1]), cols]
        term = jnp.dot(attended, rows, preferred_element_type=jnp.float32)
        total = term if total is None else total + term
    out[...] = total.astype(out.dtype)


def project(seq, width, other, parts, w, start, n, dtype):
    return pl.pallas_call(
        functools.partial(project_kernel, seq, width, other, start, len(parts)),
        out_shape=jax.ShapeDtypeStruct((parts[0].shape[0], n), dtype),
        in_specs=[inside()] * (len(parts) + 1),
        out_specs=inside(),
        compiler_params=pltpu.CompilerParams(vmem_limit_bytes=8 << 20),
        name="project",
    )(*parts, w)


def finish_kernel(n_pieces, order, own, w_mine, w_near, *refs):
    pieces, theirs, (out, attended, made, sems) = refs[:n_pieces], refs[n_pieces:-4], refs[-4:]
    n = w_mine.shape[0]
    each = n * CORES // len(order)
    for i, place in enumerate(order):
        per = len(order) // n_pieces
        at = slice(i % per * each, (i % per + 1) * each)
        attended[:, place * each : (place + 1) * each] = pieces[i // per][:, at]
    core = lax.rem(lax.axis_index("seq"), CORES)
    mine = attended[:, pl.ds(pl.multiple_of(core * n, n), n)]
    near = attended[:, pl.ds(pl.multiple_of((1 - core) * n, n), n)]
    start, copies = 0, []
    for piece in theirs:
        step = theirs[0].shape[1]
        for first in range(0, piece.shape[1], step):
            at = slice(start, start + step)
            total = own[:, at] + piece[:, first : first + step].astype(jnp.float32)
            total += jnp.dot(mine, w_mine[:, at], preferred_element_type=jnp.float32)
            total += jnp.dot(near, w_near[:, at], preferred_element_type=jnp.float32)
            made[:, at] = total.astype(made.dtype)
            copy = pltpu.make_async_copy(made.at[:, at], out.at[:, at], sems.at[len(copies)])
            copy.start()
            copies.append(copy)
            start += step
    for copy in copies:
        copy.wait()


def finish(own, attended, order, w_mine, w_near, theirs):
    return pl.pallas_call(
        functools.partial(finish_kernel, len(attended), tuple(order)),
        out_shape=jax.ShapeDtypeStruct(own.shape, jnp.bfloat16),
        in_specs=[inside()] * (3 + len(attended) + len(theirs)),
        out_specs=outside(),
        scratch_shapes=[
            pltpu.VMEM((own.shape[0], w_mine.shape[0] * CORES), jnp.bfloat16),
            pltpu.VMEM(own.shape, jnp.bfloat16),
            pltpu.SemaphoreType.DMA((own.shape[1] // theirs[0].shape[1],)),
        ],
        compiler_params=pltpu.CompilerParams(vmem_limit_bytes=8 << 20),
        name="finish",
    )(own, w_mine, w_near, *attended, *theirs)


def dealt_plan(
    seq, queries, block_keys, block_values, cache_keys, cache_values, cache_lengths, out_weight
):
    tokens, slots = queries.shape[0], cache_keys.shape[0]
    width = queries.shape[1] // GROUPS
    late = DH
    early = width - late
    stride = seq // GROUPS

    def over(x, flip):
        return lax.ppermute(x, "seq", [(s, s ^ flip) for s in range(seq)])

    def over_z(x, step):
        return over(x, step * stride)

    def over_x(x):
        return lax.ppermute(x, "head", [(0, 1), (1, 0)])

    (own_kv, own_q), first, last = pack(
        seq, width, late, cache_lengths, queries, block_keys, block_values, cache_keys, cache_values
    )
    steps = range(1, GROUPS)
    kvs = [over_z(first[2 * j - 2], j) for j in steps]
    qs = [over_z(first[2 * j - 1], j) for j in steps]
    ends = [over_z(last[j - 1], j) for j in steps]
    shipped = stage(seq, width, early, late, GROUPS // CORES, True, True, out_weight)
    w_mine = over_x(shipped)
    w_near = over(w_mine, 1)
    held_kv, held_q = hold(own_kv, own_q)
    gathered = []
    for i, kv in enumerate([own_kv] + kvs):
        far = over(kv, CORES)
        near, across = over(kv, 1), over(far, 1)
        gathered += [held_kv if i == 0 else kv, near, far, across]
    owns = gathered[:4]
    n = len(gathered)
    far_parts, kept = gather_and_attend(
        gathered + qs[1:],
        [(i, 0, 0) for i in range(n)],
        [(n, 0, 0), (n + 1, 0, 0)],
        early,
        tokens,
        slots,
    )
    near_parts = attend(kept, [held_q, qs[0]], [(0, 0, 0), (1, 0, 0)], tokens)
    parts = [near_parts[0], over_z(near_parts[1], 1)]
    parts += [over_z(far_parts[j], j + 2) for j in range(2)]
    rows = 2 * tokens + 2 * slots
    joined = join(0, ends[1:], rows)
    pieces = []
    for piece in (ends[0], joined):
        far = over(piece, CORES)
        near, across = over(piece, 1), over(far, 1)
        pieces += [piece, near, far, across]
    places = [(i, 0, early) for i in range(4)] + [(4 + i, 0, 0) for i in range(4)]
    places += [(8 + i, j * rows, 0) for j in range(GROUPS - 2) for i in range(4)]
    end_parts, _ = gather_and_attend(
        owns + pieces + [held_q] + ends[1:],
        places,
        [(12, 0, early), (4, rows, 0)] + [(13 + j, rows, 0) for j in range(GROUPS - 2)],
        late,
        tokens,
        slots,
        kept[2],
    )
    end_parts = [end_parts[0]] + [over_z(end_parts[j], j) for j in steps]
    half = out_weight.shape[1] // 2
    cuts = [0, half // 4, half]
    arrived = []
    for i in range(len(cuts) - 1):
        theirs = project(
            seq, width, True, parts, out_weight, cuts[i], cuts[i + 1] - cuts[i], jnp.bfloat16
        )
        arrived.append(over_x(theirs))
    order = (0, SOON, *(j for j in steps if j != SOON))
    attended = []
    for i in range(2):
        ending = join(1, [end_parts[j] for j in order[2 * i : 2 * i + 2]], late)
        attended.append(over_x(ending))
    both = [p for pair in zip(parts, end_parts) for p in pair]
    own = project(seq, width, False, both, out_weight, 0, half, jnp.float32)
    return finish(own, attended, order, w_mine, w_near, arrived)


def on_device(seq, head, *args):
    queries, cache_keys = args[0], args[3]
    heads_here = queries.shape[1] // DH
    slots = cache_keys.shape[0]
    rows_y = seq // (GROUPS * CORES)
    fits = (
        head == 2
        and seq % (GROUPS * CORES) == 0
        and rows_y == 2
        and heads_here % GROUPS == 0
        and heads_here > GROUPS
        and slots == 16
        and (seq * slots) % 128 == 0
        and queries.shape[0] % 16 == 0
        and args[6].shape[1] % 1024 == 0
    )
    return dealt_plan(seq, *args) if fits else gathered_plan(*args)


def solution(mesh):
    return jax.shard_map(
        functools.partial(on_device, mesh.shape["seq"], mesh.shape["head"]),
        mesh=mesh,
        in_specs=(
            P("seq", "head"),
            P("seq", "head"),
            P("seq", "head"),
            P("seq", "head"),
            P("seq", "head"),
            P("seq"),
            P("head", None),
        ),
        out_specs=P("seq", "head"),
        check_vma=False,
    )
```
